256 devices in a mesh: row: 32 (over x, y, core), col: 8 (over z).
Axes of the slice: x: 4, y: 4, z: 8, core: 2. Of those that a mesh axis runs over, the one named last changes fastest.
Arguments:
- tile_values: bfloat16 [24576, 256, 256], P(('row', 'col')), may hold values from -0.375 to 0.375
- tile_coords: int32 [24576, 2], P(('row', 'col')), may hold values from 0 to 15, as said below
- live_counts: int32 [256], P(('row', 'col')), may hold values from 24 to 96, as said below
Outputs:
- range_basis: float32 [131072, 192], P(('row', 'col'))
- projected: float32 [8, 4096, 192], P('col', 'row')
The draws below stay inside these ranges and needn't reach their ends.
Inputs may be any that keep to these rules, and one draw needn't show every extreme that they name: `tile_coords`: for each device, column 0 is below 16, column 1 is below 16, and the 96 positions of its slots are distinct. `live_counts`: some device has all 96 slots live.
All inputs are finite; a program needn't handle non-finite values.
Results may differ from the reference program's by a relative error of at most 0.0003.
Values sent between devices are 32-bit elements; how exact they have to be, the bound alone decides.
No kernel may reach another device: no remote copies, remote signals or barrier semaphores. Data moves between devices by JAX's collectives and lax.ppermute only.
A program may use at most 128 MiB of HBM per device.

```python
import math
import jax
import jax.numpy as jnp
from jax import lax

TB = 256
K = 192
RT = 16
CT = 16
NT = 96
M = 131072
N_ROW = 32
N_COL = 8


def draw_tile_values(key, part):
    device_total = N_ROW * N_COL
    base_key = jax.random.fold_in(key, 11)

    def device_draw(device_id):
        device_key = jax.random.fold_in(base_key, device_id)
        block = jnp.clip(0.125 + 0.0625 * jax.random.normal(device_key, (NT, TB, TB), jnp.float32), -0.375, 0.375)
        return block.astype(jnp.bfloat16)
    drawn = lax.map(device_draw, jnp.arange(device_total, dtype=jnp.int32))
    return drawn.reshape(device_total * NT, TB, TB)


def draw_tile_coords(key, part):
    device_total = N_ROW * N_COL
    device_keys = jax.random.split(key, device_total)

    def device_draw(device_key):
        ordering = jax.random.permutation(device_key, RT * CT)[:NT].astype(jnp.int32)
        return jnp.stack([ordering // CT, ordering % CT], axis=1).astype(jnp.int32)
    return jax.vmap(device_draw)(device_keys).reshape(device_total * NT, 2)


def draw_live_counts(key, part):
    device_total = N_ROW * N_COL
    counts_drawn = jax.random.randint(key, (device_total,), max(1, NT // 4), NT + 1, dtype=jnp.int32)
    chosen = jax.random.randint(jax.random.fold_in(key, 7), (), 0, device_total, dtype=jnp.int32)
    return counts_drawn.at[chosen].set(NT)


def setup_inputs(seed: int = 0) -> dict:
    key_of = jax.random.split(jax.random.key(seed), 4)
    tile_values = draw_tile_values(jax.random.fold_in(key_of[3], 71), 0)
    tile_coords = draw_tile_coords(jax.random.fold_in(key_of[3], 71), 0)
    live_counts = draw_live_counts(jax.random.fold_in(key_of[3], 71), 0)
    return {"tile_values": tile_values, "tile_coords": tile_coords, "live_counts": live_counts}


def sketch_signs(column_ids, rank_cols):
    rank_index = jnp.arange(rank_cols, dtype=jnp.int32)
    hashed = column_ids[..., None] * rank_cols + rank_index
    hashed = hashed * 747796405 + 1442695040
    hashed = hashed ^ hashed >> 15
    hashed = hashed * 1103515245 + 12345
    hashed = hashed ^ hashed >> 13
    return (1 - 2 * (hashed >> 9 & 1)).astype(jnp.float32)

def reference(tile_values, tile_coords, live_counts):
    device_total = N_ROW * N_COL
    values = tile_values.reshape(device_total, NT, TB, TB)
    coords = tile_coords.reshape(device_total, NT, 2)
    device_ids = jnp.arange(device_total, dtype=jnp.int32)
    slot_ids = jnp.arange(NT, dtype=jnp.int32)

    def sketch_step(running, inputs):
        tile_block, slot_coords, live_total, device_id = inputs
        row_dev = device_id // N_COL
        col_dev = device_id % N_COL
        live_mask = (slot_ids < live_total).astype(jnp.float32)[:, None, None]
        column_ids = col_dev * (CT * TB) + slot_coords[:, 1:2] * TB + jnp.arange(TB, dtype=jnp.int32)[None, :]
        test_signs = sketch_signs(column_ids, K)
        tile_terms = jnp.einsum('tij,tjk->tik', tile_block.astype(jnp.float32), test_signs, precision=lax.Precision.HIGHEST) * live_mask
        row_ids = row_dev * RT + slot_coords[:, 0]
        return (running.at[row_ids].add(tile_terms), None)
    start = jnp.zeros((RT * N_ROW, TB, K), jnp.float32)
    sketch, _ = lax.scan(sketch_step, start, (values, coords, live_counts, device_ids))
    sketch = sketch.reshape(M, K)
    gram_matrix = jnp.dot(sketch.T.astype(jnp.float32), sketch.astype(jnp.float32), precision=lax.Precision.HIGHEST, preferred_element_type=jnp.float32)
    factor = jnp.linalg.cholesky(gram_matrix)
    solved = jax.scipy.linalg.solve_triangular(factor, sketch.T, lower=True)
    range_basis = math.sqrt(M) * solved.T
    basis_blocks = range_basis.reshape(RT * N_ROW, TB, K)

    def adjoint_step(running, inputs):
        tile_block, slot_coords, live_total, device_id = inputs
        row_dev = device_id // N_COL
        col_dev = device_id % N_COL
        live_mask = (slot_ids < live_total).astype(jnp.float32)[:, None, None]
        picked = basis_blocks[row_dev * RT + slot_coords[:, 0]]
        tile_terms = jnp.einsum('tij,tik->tjk', tile_block.astype(jnp.float32), picked, precision=lax.Precision.HIGHEST) * live_mask
        col_ids = col_dev * CT + slot_coords[:, 1]
        return (running.at[col_ids].add(tile_terms), None)
    begin = jnp.zeros((CT * N_COL, TB, K), jnp.float32)
    projected, _ = lax.scan(adjoint_step, begin, (values, coords, live_counts, device_ids))
    return (range_basis, projected.reshape(N_COL, CT * TB, K))
```

```python
import functools
import math

import jax
import jax.numpy as jnp
from jax import lax
from jax.experimental import pallas as pl
from jax.experimental.pallas import tpu as pltpu
from jax.sharding import Mesh
from jax.sharding import PartitionSpec as P

TB = 256
K = 192
RT = 16
CT = 16
NT = 96
NZ = 8
KH = K // 2
CH = RT * TB // NZ
SLOTS = 8
STEPS = NT // SLOTS
HIGHEST = lax.Precision.HIGHEST


def dot_nt(a, b, precision=None):
    return lax.dot_general(
        a, b, (((1,), (1,)), ((), ())), precision=precision, preferred_element_type=jnp.float32
    )


def dot_nn(a, b, precision=None):
    return lax.dot_general(
        a, b, (((1,), (0,)), ((), ())), precision=precision, preferred_element_type=jnp.float32
    )


def sketch_body(meta_ref, live_ref, pos_ref, tiles_ref, *refs):
    outs = refs[: 2 * NZ]
    omega_ref, acc_ref = refs[2 * NZ :]
    step = pl.program_id(0)

    @pl.when(step == 0)
    def _():
        k_ids = lax.broadcasted_iota(jnp.int32, (K, TB), 0)
        g_ids = lax.broadcasted_iota(jnp.int32, (K, TB), 1)
        base = g_ids * K + k_ids
        z = pos_ref[0]

        def fill(j, carry):
            h = base + (z * CT + j) * (TB * K)
            h = h * 747796405 + 1442695040
            h = h ^ (h >> 15)
            h = h * 1103515245 + 12345
            h = h ^ (h >> 13)
            omega_ref[j] = (1 - 2 * ((h >> 9) & 1)).astype(jnp.float32).astype(jnp.bfloat16)
            return carry

        lax.fori_loop(0, CT, fill, 0)

        def clear(i, carry):
            acc_ref[i] = jnp.zeros((K, TB), jnp.float32)
            return carry

        lax.fori_loop(0, RT + 1, clear, 0)

    @pl.when(step * SLOTS < live_ref[0])
    def _():
        for t in range(SLOTS):
            code = meta_ref[step * SLOTS + t]
            i = code >> 4
            j = code & 15
            acc_ref[i] += dot_nt(omega_ref[j], tiles_ref[t])

    @pl.when(step == STEPS - 1)
    def _():
        for d in range(NZ):
            for half in range(2):
                for e in range(2):
                    outs[half * NZ + d][:, e * TB : (e + 1) * TB] = acc_ref[
                        2 * d + e, half * KH : (half + 1) * KH, :
                    ]


def tile_block(step, meta, live, pos):
    return (jnp.minimum(step, (live[0] - 1) // SLOTS), 0, 0)


def whole(shape):
    return pl.BlockSpec(shape, lambda *_: (0,) * len(shape))


def sketch_call(meta, live, pos, tiles):
    shape = (KH, CH)
    return pl.pallas_call(
        sketch_body,
        name="sketch",
        grid_spec=pltpu.PrefetchScalarGridSpec(
            num_scalar_prefetch=3,
            grid=(STEPS,),
            in_specs=[pl.BlockSpec((SLOTS, TB, TB), tile_block)],
            out_specs=[whole(shape)] * (2 * NZ),
            scratch_shapes=[
                pltpu.VMEM((CT, K, TB), jnp.bfloat16),
                pltpu.VMEM((RT + 1, K, TB), jnp.float32),
            ],
        ),
        out_shape=[jax.ShapeDtypeStruct(shape, jnp.float32)] * (2 * NZ),
        compiler_params=pltpu.CompilerParams(vmem_limit_bytes=32 << 20),
    )(meta, live, pos, tiles)


def adjoint_body(meta_ref, live_ref, pos_ref, tiles_ref, *refs):
    chunks = refs[: 2 * NZ]
    keep_ref, give_ref, gkeep_ref, ggive_ref, split_ref, acc_ref, gram_ref = refs[2 * NZ :]
    step = pl.program_id(0)
    core = pos_ref[1]

    @pl.when(step == 0)
    def _():
        for d in range(NZ):
            for half in range(2):
                for e in range(2):
                    full = chunks[half * NZ + d][:, e * TB : (e + 1) * TB]
                    high = full.astype(jnp.bfloat16)
                    low = (full - high.astype(jnp.float32)).astype(jnp.bfloat16)
                    row = half * KH
                    split_ref[2 * d + e, row : row + KH, :] = high
                    split_ref[2 * d + e, K + row : K + row + KH, :] = low

        def clear(j, carry):
            acc_ref[j] = jnp.zeros((K, TB), jnp.float32)
            return carry

        lax.fori_loop(0, CT + 1, clear, 0)
        gram = jnp.zeros((2 * K, K), jnp.float32)
        for i in range(RT):
            gram += dot_nt(split_ref[i], split_ref[i, :K, :])
        cross = gram[K:]
        gram_ref[...] = gram[:K] + (cross + cross.T)
        gkeep_ref[...] = gram_ref[pl.ds(core * KH, KH), :]
        ggive_ref[...] = gram_ref[pl.ds((1 - core) * KH, KH), :]

    @pl.when(step * SLOTS < live_ref[0])
    def _():
        for t in range(SLOTS):
            code = meta_ref[step * SLOTS + t]
            i = (code >> 4) & 15
            jx = ((code >> 2) - pos_ref[2]) & 3
            jy = (code - pos_ref[3]) & 3
            j = jnp.where(code >= RT * CT, CT, jx * 4 + jy)
            part = dot_nn(split_ref[i], tiles_ref[t])
            acc_ref[j] += part[:K] + part[K:]

    @pl.when(step == STEPS - 1)
    def _():
        mine = pl.multiple_of(core * 128, 128)
        other = pl.multiple_of((1 - core) * 128, 128)
        for j in range(CT):
            keep_ref[j] = acc_ref[j, :, pl.ds(mine, 128)]
            give_ref[j] = acc_ref[j, :, pl.ds(other, 128)]


def adjoint_call(meta, live, pos, tiles, chunks):
    shape = (KH, CH)
    part = (CT, K, 128)
    return pl.pallas_call(
        adjoint_body,
        name="adjoint",
        grid_spec=pltpu.PrefetchScalarGridSpec(
            num_scalar_prefetch=3,
            grid=(STEPS,),
            in_specs=[pl.BlockSpec((SLOTS, TB, TB), tile_block)] + [whole(shape)] * (2 * NZ),
            out_specs=[whole(part), whole(part), whole((KH, K)), whole((KH, K))],
            scratch_shapes=[
                pltpu.VMEM((RT, 2 * K, TB), jnp.bfloat16),
                pltpu.VMEM((CT + 1, K, TB), jnp.float32),
                pltpu.VMEM((K, K), jnp.float32),
            ],
        ),
        out_shape=[
            jax.ShapeDtypeStruct(part, jnp.float32),
            jax.ShapeDtypeStruct(part, jnp.float32),
            jax.ShapeDtypeStruct((KH, K), jnp.float32),
            jax.ShapeDtypeStruct((KH, K), jnp.float32),
        ],
        compiler_params=pltpu.CompilerParams(vmem_limit_bytes=48 << 20),
    )(meta, live, pos, tiles, *chunks)


NB = 64


def inverse_factor(block, rows_ref):
    eye = (
        lax.broadcasted_iota(jnp.int32, (NB, NB), 0) == lax.broadcasted_iota(jnp.int32, (NB, NB), 1)
    ).astype(jnp.float32)
    work = jnp.concatenate([eye, block], axis=1)
    first = 0
    for k in range(0, NB, 2):
        o = k - first
        rows = NB - first
        a = jnp.broadcast_to(work[:, NB + k : NB + k + 1], (rows, 2 * NB))
        b = jnp.broadcast_to(work[:, NB + k + 1 : NB + k + 2], (rows, 2 * NB))
        p = a[o : o + 1]
        q = a[o + 1 : o + 2]
        r = b[o + 1 : o + 2]
        r0 = work[o : o + 1]
        r1 = work[o + 1 : o + 2]
        inv = 1.0 / (p * r - q * q)
        u0 = (r * r0 - q * r1) * inv
        u1 = (p * r1 - q * r0) * inv
        rows_ref[k : k + 1, :] = r0 * lax.rsqrt(p)
        ratio = q / p
        rows_ref[k + 1 : k + 2, :] = (r1 - ratio * r0) * lax.rsqrt(r - ratio * q)
        if k + 2 == NB:
            break
        skip = (k + 2) // 8 * 8 - first
        if skip:
            work, a, b = work[skip:], a[skip:], b[skip:]
            first += skip
        if (k + 2) % 8:
            below = lax.broadcasted_iota(jnp.int32, a.shape, 0) >= k + 2 - first
            a = jnp.where(below, a, 0.0)
            b = jnp.where(below, b, 0.0)
        work = work - (a * u0 + b * u1)
    return rows_ref[:, :NB]


def factor_body(pos_ref, keep_ref, give_ref, out_ref, gram_ref, rows_ref, *, scale):
    core = pos_ref[1]
    gram_ref[pl.ds(core * KH, KH), :] = keep_ref[...]
    gram_ref[pl.ds((1 - core) * KH, KH), :] = give_ref[...]
    n = NB
    w0 = inverse_factor(gram_ref[:n, :n], rows_ref)
    panel = dot_nt(gram_ref[n:, :n], w0, HIGHEST)
    trail = gram_ref[n:, n:] - dot_nt(panel, panel, HIGHEST)
    w1 = inverse_factor(trail[:n, :n], rows_ref)
    l21 = dot_nt(trail[n:, :n], w1, HIGHEST)
    w2 = inverse_factor(trail[n:, n:] - dot_nt(l21, l21, HIGHEST), rows_ref)
    x10 = -dot_nn(w1, dot_nn(panel[:n], w0, HIGHEST), HIGHEST)
    x21 = -dot_nn(w2, dot_nn(l21, w1, HIGHEST), HIGHEST)
    x20 = -dot_nn(w2, dot_nn(panel[n:], w0, HIGHEST) + dot_nn(l21, x10, HIGHEST), HIGHEST)
    out_ref[...] = jnp.zeros((K, K), jnp.float32)
    out_ref[:n, :n] = w0 * scale
    out_ref[n : 2 * n, :n] = x10 * scale
    out_ref[n : 2 * n, n : 2 * n] = w1 * scale
    out_ref[2 * n :, :n] = x20 * scale
    out_ref[2 * n :, n : 2 * n] = x21 * scale
    out_ref[2 * n :, 2 * n :] = w2 * scale


def factor_call(pos, keep, give, scale):
    return pl.pallas_call(
        functools.partial(factor_body, scale=scale),
        name="factor",
        in_specs=[
            pl.BlockSpec(memory_space=pltpu.SMEM),
            pl.BlockSpec(memory_space=pltpu.VMEM),
            pl.BlockSpec(memory_space=pltpu.VMEM),
        ],
        out_specs=pl.BlockSpec(memory_space=pltpu.VMEM),
        scratch_shapes=[pltpu.VMEM((K, K), jnp.float32), pltpu.VMEM((NB, 2 * NB), jnp.float32)],
        out_shape=jax.ShapeDtypeStruct((K, K), jnp.float32),
    )(pos, keep, give)


def apply_body(factor_ref, top_ref, bottom_ref, out_ref):
    both = jnp.concatenate([top_ref[...], bottom_ref[...]], axis=0)
    out_ref[...] = dot_nn(factor_ref[...], both, HIGHEST).T


def apply_call(factor, top, bottom, name):
    return pl.pallas_call(
        apply_body,
        name=name,
        out_shape=jax.ShapeDtypeStruct((top.shape[1], K), jnp.float32),
    )(factor, top, bottom)


def shift(x, axis, size, by):
    return lax.ppermute(x, axis, [(i, (i + by) % size) for i in range(size)])


def reduce_z(parts):
    chains = []
    for half, part in enumerate(parts):
        up, down = (4, 3) if half == 0 else (3, 4)
        chains.append([part[up], part[NZ - down], up, down])
    for _ in range(4):
        for chain, part in zip(chains, parts):
            if chain[2]:
                chain[0] = shift(chain[0], "z", NZ, 1)
                chain[2] -= 1
                if chain[2]:
                    chain[0] = chain[0] + part[chain[2]]
            if chain[3]:
                chain[1] = shift(chain[1], "z", NZ, -1)
                chain[3] -= 1
                if chain[3]:
                    chain[1] = chain[1] + part[NZ - chain[3]]
    return [chain[0] + chain[1] + part[0] for chain, part in zip(chains, parts)]


def gather_z(own):
    found = [[mine] + [None] * (NZ - 1) for mine in own]
    for step in range(1, 5):
        for half, got in enumerate(found):
            if step <= (4 if half == 0 else 3):
                got[NZ - step] = shift(got[(NZ - step + 1) % NZ], "z", NZ, 1)
            if step <= (3 if half == 0 else 4):
                got[step] = shift(got[step - 1], "z", NZ, -1)
    return found


def exchange(blocks, axis):
    total = blocks[0]
    for d in range(1, 4):
        total = total + shift(blocks[d], axis, 4, d)
    return total


def sum_ring(x, axis):
    return exchange([x] * 4, axis)


def scatter_xy(blocks):
    grid = blocks.reshape(4, 4, K, 128)
    a = exchange([grid[d, :, :KH] for d in range(4)], "x")
    b = exchange([grid[:, d, KH:] for d in range(4)], "y")
    a = exchange([a[d] for d in range(4)], "y")
    b = exchange([b[d] for d in range(4)], "x")
    return a, b


def per_device(tile_values, tile_coords, live_counts):
    x, y, core, z = (lax.axis_index(name).astype(jnp.int32) for name in ("x", "y", "core", "z"))
    pos = jnp.stack([z, core, x, y])
    live = jnp.arange(NT, dtype=jnp.int32) < live_counts[0]
    relative = (tile_coords[:, 0] - 2 * z) & (RT - 1)
    meta = jnp.where(live, relative, RT) * CT + tile_coords[:, 1]
    parts = sketch_call(meta, live_counts, pos, tile_values)
    own = reduce_z([parts[:NZ], parts[NZ:]])
    found = gather_z(own)
    keep, give, gkeep, ggive = adjoint_call(meta, live_counts, pos, tile_values, found[0] + found[1])
    gram = gkeep + shift(ggive, "core", 2, 1)
    gram = sum_ring(sum_ring(gram, "x"), "y")
    scale = math.sqrt(RT * TB * 32)
    factor = factor_call(pos, gram, shift(gram, "core", 2, 1), scale)
    range_basis = apply_call(factor, own[0], own[1], "basis")
    low, high = scatter_xy(keep + shift(give, "core", 2, 1))
    projected = apply_call(factor, low, high, "project")
    return range_basis, projected[None]


def solution(mesh):
    split = Mesh(mesh.devices.reshape(4, 4, 2, NZ), ("x", "y", "core", "z"))
    row = ("x", "y", "core")
    both = (*row, "z")
    in_specs = (P(both, None, None), P(both, None), P(both))
    out_specs = (P(both, None), P("z", row, None))
    return jax.shard_map(
        per_device, mesh=split, in_specs=in_specs, out_specs=out_specs, check_vma=False
    )
```

```python
import functools
import math

import jax
import jax.numpy as jnp
from jax import lax
from jax.experimental import pallas as pl
from jax.experimental.pallas import tpu as pltpu
from jax.sharding import Mesh
from jax.sharding import PartitionSpec as P

TB = 256
K = 192
RT = 16
CT = 16
NT = 96
NZ = 8
KH = K // 2
CH = RT * TB // NZ
SLOTS = 8
STEPS = NT // SLOTS
HIGHEST = lax.Precision.HIGHEST


def dot_nt(a, b, precision=None):
    return lax.dot_general(
        a, b, (((1,), (1,)), ((), ())), precision=precision, preferred_element_type=jnp.float32
    )


def dot_nn(a, b, precision=None):
    return lax.dot_general(
        a, b, (((1,), (0,)), ((), ())), precision=precision, preferred_element_type=jnp.float32
    )


SMEM_SPEC = pl.BlockSpec(memory_space=pltpu.SMEM)
VMEM_SPEC = pl.BlockSpec(memory_space=pltpu.VMEM)
HBM_SPEC = pl.BlockSpec(memory_space=pltpu.HBM)


def sketch_body(meta_ref, live_ref, pos_ref, tiles_ref, *refs):
    outs = refs[: 2 * NZ]
    omega_ref, acc_ref, buf_ref, sems = refs[2 * NZ :]
    steps = (live_ref[0] + SLOTS - 1) >> 3

    def copy(step):
        return pltpu.make_async_copy(
            tiles_ref.at[pl.ds(step * SLOTS, SLOTS)],
            buf_ref.at[pl.ds(step * SLOTS, SLOTS)],
            sems.at[step],
        )

    def fetch(step, carry):
        copy(step).start()
        return carry

    lax.fori_loop(0, steps, fetch, 0)
    k_ids = lax.broadcasted_iota(jnp.int32, (K, TB), 0)
    g_ids = lax.broadcasted_iota(jnp.int32, (K, TB), 1)
    base = g_ids * K + k_ids
    z = pos_ref[0]

    def fill(j, carry):
        h = base + (z * CT + j) * (TB * K)
        h = h * 747796405 + 1442695040
        h = h ^ (h >> 15)
        h = h * 1103515245 + 12345
        h = h ^ (h >> 13)
        omega_ref[j] = (1 - 2 * ((h >> 9) & 1)).astype(jnp.float32).astype(jnp.bfloat16)
        acc_ref[j] = jnp.zeros((K, TB), jnp.float32)
        return carry

    lax.fori_loop(0, CT, fill, 0)

    def work(step, carry):
        copy(step).wait()
        for t in range(SLOTS):
            slot = step * SLOTS + t
            code = meta_ref[slot]
            acc_ref[code >> 4] += dot_nt(omega_ref[code & 15], buf_ref[slot])
        return carry

    lax.fori_loop(0, steps, work, 0)
    for d in range(NZ):
        for half in range(2):
            for e in range(2):
                outs[half * NZ + d][:, e * TB : (e + 1) * TB] = acc_ref[
                    2 * d + e, half * KH : (half + 1) * KH, :
                ]


def sketch_call(meta, live, pos, tiles):
    return pl.pallas_call(
        sketch_body,
        name="sketch",
        in_specs=[SMEM_SPEC, SMEM_SPEC, SMEM_SPEC, HBM_SPEC],
        out_specs=[VMEM_SPEC] * (2 * NZ),
        scratch_shapes=[
            pltpu.VMEM((CT, K, TB), jnp.bfloat16),
            pltpu.VMEM((RT + 1, K, TB), jnp.float32),
            pltpu.VMEM((NT, TB, TB), jnp.bfloat16),
            pltpu.SemaphoreType.DMA((STEPS,)),
        ],
        out_shape=[jax.ShapeDtypeStruct((KH, CH), jnp.float32)] * (2 * NZ),
        compiler_params=pltpu.CompilerParams(vmem_limit_bytes=40 << 20),
    )(meta, live, pos, tiles)


NEAR = (0, 1, 2, 6, 7)
FAR = (3, 4, 5)


def adjoint_body(order_ref, meta_ref, count_ref, pos_ref, tiles_ref, *refs, dists, last):
    chunks = refs[: 2 * len(dists)]
    refs = refs[2 * len(dists) :]
    if last:
        acc_in, gram_in, keep_ref, give_ref = refs[:4]
    else:
        acc_out, gram_out = refs[:2]
    split_ref, acc_ref, gram_ref, buf_ref, sems = refs[-5:]
    first = count_ref[0] if last else 0
    total = count_ref[1] if last else count_ref[0]
    unroll = SLOTS if last else SLOTS // 2
    steps = (total + unroll - 1) >> (3 if last else 2)
    core = pos_ref[1]

    def copy(step, t):
        rank = step * unroll + t
        slot = order_ref[jnp.minimum(first + rank, NT - 1)]
        return pltpu.make_async_copy(tiles_ref.at[slot], buf_ref.at[rank], sems.at[step])

    def fetch(step, carry):
        for t in range(unroll):
            copy(step, t).start()
        return carry

    lax.fori_loop(0, steps, fetch, 0)
    for c, d in enumerate(dists):
        for half in range(2):
            for e in range(2):
                full = chunks[half * len(dists) + c][:, e * TB : (e + 1) * TB]
                high = full.astype(jnp.bfloat16)
                low = (full - high.astype(jnp.float32)).astype(jnp.bfloat16)
                row = half * KH
                split_ref[2 * c + e, row : row + KH, :] = high
                split_ref[2 * c + e, K + row : K + row + KH, :] = low
    gram_ref[...] = jnp.zeros((2 * K, K), jnp.float32)

    def square(i, carry):
        gram_ref[...] += dot_nt(split_ref[i], split_ref[i, :K, :])
        return carry

    lax.fori_loop(0, 2 * len(dists), square, 0)
    cross = gram_ref[K:, :]
    gram = gram_ref[:K, :] + (cross + cross.T)
    if last:
        gram = gram_in[...] + gram
        low, high = gram[:, :KH], gram[:, KH:]
        keep_ref[CT] = jnp.zeros((K, 128), jnp.float32)
        give_ref[CT] = jnp.zeros((K, 128), jnp.float32)
        keep_ref[CT, :, :KH] = jnp.where(core == 1, high, low)
        give_ref[CT, :, :KH] = jnp.where(core == 1, low, high)
    else:
        gram_out[...] = gram

    def clear(j, carry):
        acc_ref[j] = acc_in[j] if last else jnp.zeros((K, TB), jnp.float32)
        return carry

    lax.fori_loop(0, CT, clear, 0)

    def work(step, carry):
        for t in range(unroll):
            copy(step, t).wait()
        for t in range(unroll):
            rank = step * unroll + t
            code = meta_ref[order_ref[jnp.minimum(first + rank, NT - 1)]]
            i = place_of((code >> 4) & 15, dists)
            j = jnp.where(rank < total, code & 15, CT)
            part = dot_nn(split_ref[i], buf_ref[rank])
            acc_ref[j] += part[:K] + part[K:]
        return carry

    lax.fori_loop(0, steps, work, 0)
    if last:
        mine = pl.multiple_of(core * 128, 128)
        other = pl.multiple_of((1 - core) * 128, 128)

        def place(q, carry):
            one = q >> 2
            two = q & 3
            swap = core == 1
            own = chip_of(pos_ref, jnp.where(swap, two, one), jnp.where(swap, one, two))
            far = chip_of(pos_ref, jnp.where(swap, one, two), jnp.where(swap, two, one))
            keep_ref[q] = acc_ref[own, :, pl.ds(mine, 128)]
            give_ref[q] = acc_ref[far, :, pl.ds(other, 128)]
            return carry

        lax.fori_loop(0, CT, place, 0)
    else:

        def save(j, carry):
            acc_out[j] = acc_ref[j]
            return carry

        lax.fori_loop(0, CT, save, 0)


def place_of(i, dists):
    if dists == FAR:
        return jnp.clip(i - 2 * FAR[0], 0, 2 * len(FAR) - 1)
    return jnp.clip(jnp.where(i >= 12, i - 6, i), 0, 2 * len(NEAR) - 1)


def chip_of(pos_ref, dx, dy):
    return ((pos_ref[2] + dx) & 3) * 4 + ((pos_ref[3] + dy) & 3)


def adjoint_call(order, meta, count, pos, tiles, chunks, dists, carried=()):
    last = bool(carried)
    part = (CT + 1, K, 128)
    outs = [part, part] if last else [(CT, K, TB), (K, K)]
    return pl.pallas_call(
        functools.partial(adjoint_body, dists=dists, last=last),
        name="adjoint_far" if last else "adjoint_near",
        in_specs=[SMEM_SPEC] * 4 + [HBM_SPEC] + [VMEM_SPEC] * (len(chunks) + len(carried)),
        out_specs=[VMEM_SPEC] * len(outs),
        scratch_shapes=[
            pltpu.VMEM((2 * len(dists), 2 * K, TB), jnp.bfloat16),
            pltpu.VMEM((CT + 1, K, TB), jnp.float32),
            pltpu.VMEM((2 * K, K), jnp.float32),
            pltpu.VMEM((NT, TB, TB), jnp.bfloat16),
            pltpu.SemaphoreType.DMA((2 * STEPS,)),
        ],
        out_shape=[jax.ShapeDtypeStruct(o, jnp.float32) for o in outs],
        compiler_params=pltpu.CompilerParams(vmem_limit_bytes=40 << 20),
    )(order, meta, count, pos, tiles, *chunks, *carried)


NB = 64


def inverse_factor(block, rows_ref):
    eye = (
        lax.broadcasted_iota(jnp.int32, (NB, NB), 0) == lax.broadcasted_iota(jnp.int32, (NB, NB), 1)
    ).astype(jnp.float32)
    work = jnp.concatenate([eye, block], axis=1)
    first = 0
    for k in range(0, NB, 2):
        o = k - first
        rows = NB - first
        a = jnp.broadcast_to(work[:, NB + k : NB + k + 1], (rows, 2 * NB))
        b = jnp.broadcast_to(work[:, NB + k + 1 : NB + k + 2], (rows, 2 * NB))
        p = a[o : o + 1]
        q = a[o + 1 : o + 2]
        r = b[o + 1 : o + 2]
        r0 = work[o : o + 1]
        r1 = work[o + 1 : o + 2]
        inv = 1.0 / (p * r - q * q)
        u0 = (r * r0 - q * r1) * inv
        u1 = (p * r1 - q * r0) * inv
        rows_ref[k : k + 1, :] = r0 * lax.rsqrt(p)
        ratio = q / p
        rows_ref[k + 1 : k + 2, :] = (r1 - ratio * r0) * lax.rsqrt(r - ratio * q)
        if k + 2 == NB:
            break
        skip = (k + 2) // 8 * 8 - first
        if skip:
            work, a, b = work[skip:], a[skip:], b[skip:]
            first += skip
        if (k + 2) % 8:
            below = lax.broadcasted_iota(jnp.int32, a.shape, 0) >= k + 2 - first
            a = jnp.where(below, a, 0.0)
            b = jnp.where(below, b, 0.0)
        work = work - (a * u0 + b * u1)
    return rows_ref[:, :NB]


def factor_body(pos_ref, keep_ref, give_ref, out_ref, gram_ref, rows_ref, panel_ref, *, scale):
    core = pos_ref[1]
    mine, other = keep_ref[:, :KH], give_ref[:, :KH]
    gram_ref[:, :KH] = jnp.where(core == 1, other, mine)
    gram_ref[:, KH:] = jnp.where(core == 1, mine, other)
    n = NB
    rows_ref[3] = gram_ref[:n, : 2 * n]
    out_ref[...] = jnp.zeros((K, K), jnp.float32)

    def block(b, carry):
        w = inverse_factor(rows_ref[3, :, :n], rows_ref.at[b])

        @pl.when(b == 0)
        def _():
            panel = dot_nt(gram_ref[n:, :n], w, HIGHEST)
            panel_ref[...] = panel
            trail = gram_ref[n:, n:] - dot_nt(panel, panel, HIGHEST)
            gram_ref[n:, n:] = trail
            rows_ref[3] = trail[:n]

        @pl.when(b == 1)
        def _():
            l21 = dot_nt(gram_ref[2 * n :, n : 2 * n], w, HIGHEST)
            gram_ref[2 * n :, :n] = l21
            rows_ref[3, :, :n] = gram_ref[2 * n :, 2 * n :] - dot_nt(l21, l21, HIGHEST)

        return carry

    lax.fori_loop(0, 3, block, 0)
    w0, w1, w2 = (rows_ref[b, :, :n] for b in range(3))
    panel = panel_ref[...]
    l21 = gram_ref[2 * n :, :n]
    x10 = -dot_nn(w1, dot_nn(panel[:n], w0, HIGHEST), HIGHEST)
    x21 = -dot_nn(w2, dot_nn(l21, w1, HIGHEST), HIGHEST)
    x20 = -dot_nn(w2, dot_nn(panel[n:], w0, HIGHEST) + dot_nn(l21, x10, HIGHEST), HIGHEST)
    out_ref[:n, :n] = w0 * scale
    out_ref[n : 2 * n, :n] = x10 * scale
    out_ref[n : 2 * n, n : 2 * n] = w1 * scale
    out_ref[2 * n :, :n] = x20 * scale
    out_ref[2 * n :, n : 2 * n] = x21 * scale
    out_ref[2 * n :, 2 * n :] = w2 * scale


def factor_call(pos, keep, give, scale):
    return pl.pallas_call(
        functools.partial(factor_body, scale=scale),
        name="factor",
        in_specs=[
            pl.BlockSpec(memory_space=pltpu.SMEM),
            pl.BlockSpec(memory_space=pltpu.VMEM),
            pl.BlockSpec(memory_space=pltpu.VMEM),
        ],
        out_specs=pl.BlockSpec(memory_space=pltpu.VMEM),
        scratch_shapes=[
            pltpu.VMEM((K, K), jnp.float32),
            pltpu.VMEM((4, NB, 2 * NB), jnp.float32),
            pltpu.VMEM((2 * NB, NB), jnp.float32),
        ],
        out_shape=jax.ShapeDtypeStruct((K, K), jnp.float32),
    )(pos, keep, give)


def apply_body(factor_ref, *refs):
    out_ref = refs[-1]
    both = jnp.concatenate([r[...] for r in refs[:-1]], axis=0)
    out_ref[...] = dot_nn(factor_ref[...], both, HIGHEST)


def apply_call(factor, parts, name):
    return pl.pallas_call(
        apply_body,
        name=name,
        out_shape=jax.ShapeDtypeStruct((K, parts[0].shape[1]), jnp.float32),
    )(factor, *parts)


def shift(x, axis, size, by):
    return lax.ppermute(x, axis, [(i, (i + by) % size) for i in range(size)])


def reduce_z(parts):
    chains = []
    for half, part in enumerate(parts):
        up, down = (4, 3) if half == 0 else (3, 4)
        chains.append([part[up], part[NZ - down], up, down])
    for _ in range(4):
        for chain, part in zip(chains, parts):
            if chain[2]:
                chain[0] = shift(chain[0], "z", NZ, 1)
                chain[2] -= 1
                if chain[2]:
                    chain[0] = chain[0] + part[chain[2]]
            if chain[3]:
                chain[1] = shift(chain[1], "z", NZ, -1)
                chain[3] -= 1
                if chain[3]:
                    chain[1] = chain[1] + part[NZ - chain[3]]
    return [chain[0] + chain[1] + part[0] for chain, part in zip(chains, parts)]


def gather_z(own):
    found = [[mine] + [None] * (NZ - 1) for mine in own]
    for step in range(1, 5):
        for half, got in enumerate(found):
            if step <= (4 if half == 0 else 3):
                got[NZ - step] = shift(got[(NZ - step + 1) % NZ], "z", NZ, 1)
            if step <= (3 if half == 0 else 4):
                got[step] = shift(got[step - 1], "z", NZ, -1)
    return found


def shift_xy(x, by, stage):
    pairs = []
    for i in range(32):
        px, py, core = i // 8, i // 2 % 4, i % 2
        if core == stage:
            px = (px + by) % 4
        else:
            py = (py + by) % 4
        pairs.append((i, (px * 4 + py) * 2 + core))
    return lax.ppermute(x, ("x", "y", "core"), pairs)


def exchange(blocks, stage):
    total = blocks[0]
    for d in (2, 1, 3):
        total = total + shift_xy(blocks[d], d, stage)
    return total


def per_device(tiles, tile_coords, live_counts):
    x, y, core, z = (lax.axis_index(name).astype(jnp.int32) for name in ("x", "y", "core", "z"))
    pos = jnp.stack([z, core, x, y])
    slots = jnp.arange(NT, dtype=jnp.int32)
    live = slots < live_counts[0]
    relative = (tile_coords[:, 0] - 2 * z) & (RT - 1)
    meta = jnp.where(live, relative, RT) * CT + tile_coords[:, 1]
    parts = sketch_call(meta, live_counts, pos, tiles)
    far = (relative >= 2 * FAR[0]) & (relative < 2 * FAR[-1] + 2)
    key = jnp.where(live, far.astype(jnp.int32), 2) * NT + slots
    rank = jnp.sum((key[:, None] > key[None, :]).astype(jnp.int32), axis=1)
    order = jnp.sum(jnp.where(rank[:, None] == slots[None, :], slots[:, None], 0), axis=0)
    count = jnp.stack([jnp.sum(live & ~far), jnp.sum(live & far)]).astype(jnp.int32)
    own = reduce_z([parts[:NZ], parts[NZ:]])
    found = gather_z(own)
    near = [got[d] for got in found for d in NEAR]
    carried = adjoint_call(order, meta, count, pos, tiles, near, NEAR)
    rest = [got[d] for got in found for d in FAR]
    keep, give = adjoint_call(order, meta, count, pos, tiles, rest, FAR, carried)
    merged = keep + shift(give, "core", 2, 1)
    gram = merged[CT]
    blocks = merged[:CT].reshape(4, 4, K, 128)
    gram = exchange([gram] * 4, 0)
    blocks = exchange([blocks[d] for d in range(4)], 0)
    gram = exchange([gram] * 4, 1)
    block = exchange([blocks[d] for d in range(4)], 1)
    scale = math.sqrt(RT * TB * 32)
    factor = factor_call(pos, gram, shift(gram, "core", 2, 1), scale)
    range_basis = apply_call(factor, own, "basis")
    projected = apply_call(factor, [block], "project")
    return range_basis.T, projected.T[None]


def solution(mesh):
    split = Mesh(mesh.devices.reshape(4, 4, 2, NZ), ("x", "y", "core", "z"))
    row = ("x", "y", "core")
    both = (*row, "z")
    in_specs = (P(both, None, None), P(both, None), P(both))
    out_specs = (P(both, None), P("z", row, None))
    return jax.shard_map(
        per_device, mesh=split, in_specs=in_specs, out_specs=out_specs, check_vma=False
    )
```

```python
import functools
import math

import jax
import jax.numpy as jnp
from jax import lax
from jax.experimental import pallas as pl
from jax.experimental.pallas import tpu as pltpu
from jax.sharding import Mesh
from jax.sharding import PartitionSpec as P

TB = 256
K = 192
RT = 16
CT = 16
NT = 96
NZ = 8
KH = K // 2
CH = RT * TB // NZ
SLOTS = 8
UNROLL = 4
STEPS = NT // SLOTS
HIGHEST = lax.Precision.HIGHEST


def dot_nt(a, b, precision=None):
    return lax.dot_general(
        a, b, (((1,), (1,)), ((), ())), precision=precision, preferred_element_type=jnp.float32
    )


def dot_nn(a, b, precision=None):
    return lax.dot_general(
        a, b, (((1,), (0,)), ((), ())), precision=precision, preferred_element_type=jnp.float32
    )


SMEM_SPEC = pl.BlockSpec(memory_space=pltpu.SMEM)
VMEM_SPEC = pl.BlockSpec(memory_space=pltpu.VMEM)
HBM_SPEC = pl.BlockSpec(memory_space=pltpu.HBM)


def sketch_body(meta_ref, live_ref, pos_ref, tiles_ref, *refs):
    outs = refs[: 2 * NZ]
    omega_ref, acc_ref, buf_ref, sems = refs[2 * NZ :]
    steps = (live_ref[0] + SLOTS - 1) >> 3

    def copy(step):
        return pltpu.make_async_copy(
            tiles_ref.at[pl.ds(step * SLOTS, SLOTS)],
            buf_ref.at[pl.ds(step * SLOTS, SLOTS)],
            sems.at[step],
        )

    def fetch(step, carry):
        copy(step).start()
        return carry

    lax.fori_loop(0, steps, fetch, 0)
    k_ids = lax.broadcasted_iota(jnp.int32, (K, TB), 0)
    g_ids = lax.broadcasted_iota(jnp.int32, (K, TB), 1)
    base = g_ids * K + k_ids
    z = pos_ref[0]

    def fill(j, carry):
        h = base + (z * CT + j) * (TB * K)
        h = h * 747796405 + 1442695040
        h = h ^ (h >> 15)
        h = h * 1103515245 + 12345
        h = h ^ (h >> 13)
        omega_ref[j] = (1 - 2 * ((h >> 9) & 1)).astype(jnp.float32).astype(jnp.bfloat16)
        acc_ref[j] = jnp.zeros((K, TB), jnp.float32)
        return carry

    lax.fori_loop(0, CT, fill, 0)

    def work(step, carry):
        copy(step).wait()
        for t in range(SLOTS):
            slot = step * SLOTS + t
            code = meta_ref[slot]
            acc_ref[code >> 4] += dot_nt(omega_ref[code & 15], buf_ref[slot])
        return carry

    lax.fori_loop(0, steps, work, 0)
    for d in range(NZ):
        for half in range(2):
            for e in range(2):
                outs[half * NZ + d][:, e * TB : (e + 1) * TB] = acc_ref[
                    2 * d + e, half * KH : (half + 1) * KH, :
                ]


def sketch_call(meta, live, pos, tiles):
    return pl.pallas_call(
        sketch_body,
        name="sketch",
        in_specs=[SMEM_SPEC, SMEM_SPEC, SMEM_SPEC, HBM_SPEC],
        out_specs=[VMEM_SPEC] * (2 * NZ),
        scratch_shapes=[
            pltpu.VMEM((CT, K, TB), jnp.bfloat16),
            pltpu.VMEM((RT + 1, K, TB), jnp.float32),
            pltpu.VMEM((NT, TB, TB), jnp.bfloat16),
            pltpu.SemaphoreType.DMA((STEPS,)),
        ],
        out_shape=[jax.ShapeDtypeStruct((KH, CH), jnp.float32)] * (2 * NZ),
        compiler_params=pltpu.CompilerParams(vmem_limit_bytes=24 << 20),
    )(meta, live, pos, tiles)


NEAR = (0, 1, 2, 6, 7)
FAR = (3, 4, 5)


def split_body(*refs, n, last):
    chunks = refs[: 2 * n]
    split_ref, gram_ref, sum_ref = refs[-3:]

    for c in range(n):
        for half in range(2):
            chunk = chunks[half * n + c]

            def part(g, carry):
                rows = pl.ds(pl.multiple_of(g * 32, 32), 32)
                at = pl.multiple_of(half * KH + g * 32, 32)
                full = chunk[rows, :]
                high = full.astype(jnp.bfloat16)
                low = (full - high.astype(jnp.float32)).astype(jnp.bfloat16)
                for e in range(2):
                    cols = slice(e * TB, (e + 1) * TB)
                    split_ref[2 * c + e, pl.ds(at, 32), :] = high[:, cols]
                    split_ref[2 * c + e, pl.ds(K + at, 32), :] = low[:, cols]
                return carry

            lax.fori_loop(0, KH // 32, part, 0)
    sum_ref[...] = jnp.zeros((2 * K, K), jnp.float32)

    def square(i, carry):
        sum_ref[...] += dot_nt(split_ref[i], split_ref[i, :K, :])
        return carry

    lax.fori_loop(0, 2 * n, square, 0)
    cross = sum_ref[K:, :]
    gram = sum_ref[:K, :] + (cross + cross.T)
    if last:
        gram = refs[2 * n][...] + gram
        for row, col, (i, j) in PACKED:
            gram_ref[row : row + NB, col : col + NB] = gram[i : i + NB, j : j + NB]
    else:
        gram_ref[...] = gram


NB = 64
PACKED = (
    (0, 0, (0, 0)),
    (0, NB, (NB, 0)),
    (NB, 0, (2 * NB, 0)),
    (NB, NB, (NB, NB)),
    (2 * NB, 0, (2 * NB, 2 * NB)),
    (2 * NB, NB, (2 * NB, NB)),
)


def split_call(chunks, carried=()):
    n = len(chunks) // 2
    return pl.pallas_call(
        functools.partial(split_body, n=n, last=bool(carried)),
        name="split_far" if carried else "split_near",
        in_specs=[VMEM_SPEC] * (len(chunks) + len(carried)),
        out_specs=[VMEM_SPEC] * 2,
        scratch_shapes=[pltpu.VMEM((2 * K, K), jnp.float32)],
        out_shape=[
            jax.ShapeDtypeStruct((2 * n, 2 * K, TB), jnp.bfloat16),
            jax.ShapeDtypeStruct((K, 2 * NB) if carried else (K, K), jnp.float32),
        ],
        compiler_params=pltpu.CompilerParams(vmem_limit_bytes=8 << 20),
    )(*chunks, *carried)


def adjoint_body(order_ref, meta_ref, count_ref, pos_ref, tiles_ref, split_ref, *refs, dists, last):
    if last:
        acc_in, keep_ref, give_ref = refs[:3]
    else:
        acc_out = refs[0]
    acc_ref, buf_ref, sems = refs[-3:]
    first = count_ref[0] if last else 0
    total = count_ref[1] if last else count_ref[0]
    steps = (total + UNROLL - 1) >> 2
    core = pos_ref[1]

    def copy(step, t):
        rank = step * UNROLL + t
        slot = order_ref[jnp.minimum(first + rank, NT - 1)]
        return pltpu.make_async_copy(tiles_ref.at[slot], buf_ref.at[rank], sems.at[step])

    def fetch(step, carry):
        for t in range(UNROLL):
            copy(step, t).start()
        return carry

    lax.fori_loop(0, steps, fetch, 0)

    def clear(j, carry):
        acc_ref[j] = acc_in[j] if last else jnp.zeros((K, TB), jnp.float32)
        return carry

    lax.fori_loop(0, CT, clear, 0)

    def work(step, carry):
        for t in range(UNROLL):
            copy(step, t).wait()
        for t in range(UNROLL):
            rank = step * UNROLL + t
            code = meta_ref[order_ref[jnp.minimum(first + rank, NT - 1)]]
            i = place_of((code >> 4) & 15, dists)
            j = jnp.where(rank < total, code & 15, CT)
            part = dot_nn(split_ref[i], buf_ref[rank])
            acc_ref[j] += part[:K] + part[K:]
        return carry

    lax.fori_loop(0, steps, work, 0)
    if last:
        mine = pl.multiple_of(core * 128, 128)
        other = pl.multiple_of((1 - core) * 128, 128)

        def place(q, carry):
            one = q >> 2
            two = q & 3
            swap = core == 1
            own = chip_of(pos_ref, jnp.where(swap, two, one), jnp.where(swap, one, two))
            far = chip_of(pos_ref, jnp.where(swap, one, two), jnp.where(swap, two, one))
            keep_ref[q] = acc_ref[own, :, pl.ds(mine, 128)]
            give_ref[q] = acc_ref[far, :, pl.ds(other, 128)]
            return carry

        lax.fori_loop(0, CT, place, 0)
    else:

        def save(j, carry):
            acc_out[j] = acc_ref[j]
            return carry

        lax.fori_loop(0, CT, save, 0)


def place_of(i, dists):
    if dists == FAR:
        return jnp.clip(i - 2 * FAR[0], 0, 2 * len(FAR) - 1)
    return jnp.clip(jnp.where(i >= 12, i - 6, i), 0, 2 * len(NEAR) - 1)


def chip_of(pos_ref, dx, dy):
    return ((pos_ref[2] + dx) & 3) * 4 + ((pos_ref[3] + dy) & 3)


def adjoint_call(order, meta, count, pos, tiles, split, dists, carried=()):
    last = bool(carried)
    part = (CT, K, 128)
    outs = [part, part] if last else [(CT, K, TB)]
    return pl.pallas_call(
        functools.partial(adjoint_body, dists=dists, last=last),
        name="adjoint_far" if last else "adjoint_near",
        in_specs=[SMEM_SPEC] * 4 + [HBM_SPEC] + [VMEM_SPEC] * (1 + len(carried)),
        out_specs=[VMEM_SPEC] * len(outs),
        scratch_shapes=[
            pltpu.VMEM((CT + 1, K, TB), jnp.float32),
            pltpu.VMEM((NT, TB, TB), jnp.bfloat16),
            pltpu.SemaphoreType.DMA((NT // UNROLL,)),
        ],
        out_shape=[jax.ShapeDtypeStruct(o, jnp.float32) for o in outs],
        compiler_params=pltpu.CompilerParams(vmem_limit_bytes=24 << 20),
    )(order, meta, count, pos, tiles, split, *carried)


def inverse_factor(block, rows_ref):
    eye = (
        lax.broadcasted_iota(jnp.int32, (NB, NB), 0) == lax.broadcasted_iota(jnp.int32, (NB, NB), 1)
    ).astype(jnp.float32)
    work = jnp.concatenate([eye, block], axis=1)
    first = 0
    for k in range(0, NB, 2):
        o = k - first
        rows = NB - first
        a = jnp.broadcast_to(work[:, NB + k : NB + k + 1], (rows, 2 * NB))
        b = jnp.broadcast_to(work[:, NB + k + 1 : NB + k + 2], (rows, 2 * NB))
        p = a[o : o + 1]
        q = a[o + 1 : o + 2]
        r = b[o + 1 : o + 2]
        r0 = work[o : o + 1]
        r1 = work[o + 1 : o + 2]
        inv = 1.0 / (p * r - q * q)
        u0 = (r * r0 - q * r1) * inv
        u1 = (p * r1 - q * r0) * inv
        rows_ref[k : k + 1, :] = r0 * lax.rsqrt(p)
        ratio = q / p
        rows_ref[k + 1 : k + 2, :] = (r1 - ratio * r0) * lax.rsqrt(r - ratio * q)
        if k + 2 == NB:
            break
        skip = (k + 2) // 8 * 8 - first
        if skip:
            work, a, b = work[skip:], a[skip:], b[skip:]
            first += skip
        if (k + 2) % 8:
            below = lax.broadcasted_iota(jnp.int32, a.shape, 0) >= k + 2 - first
            a = jnp.where(below, a, 0.0)
            b = jnp.where(below, b, 0.0)
        work = work - (a * u0 + b * u1)
    return rows_ref[:, :NB]


def factor_body(packed_ref, out_ref, gram_ref, rows_ref, panel_ref, *, scale):
    n = NB
    for row, col, (i, j) in PACKED:
        block = packed_ref[row : row + n, col : col + n]
        gram_ref[i : i + n, j : j + n] = block
        if i == 2 * n and j == n:
            gram_ref[j : j + n, i : i + n] = block.T
    rows_ref[3, :, :n] = gram_ref[:n, :n]
    out_ref[...] = jnp.zeros((K, K), jnp.float32)

    def block(b, carry):
        w = inverse_factor(rows_ref[3, :, :n], rows_ref.at[b])

        @pl.when(b == 0)
        def _():
            panel = dot_nt(gram_ref[n:, :n], w, HIGHEST)
            panel_ref[...] = panel
            trail = gram_ref[n:, n:] - dot_nt(panel, panel, HIGHEST)
            gram_ref[n:, n:] = trail
            rows_ref[3] = trail[:n]

        @pl.when(b == 1)
        def _():
            l21 = dot_nt(gram_ref[2 * n :, n : 2 * n], w, HIGHEST)
            gram_ref[2 * n :, :n] = l21
            rows_ref[3, :, :n] = gram_ref[2 * n :, 2 * n :] - dot_nt(l21, l21, HIGHEST)

        return carry

    lax.fori_loop(0, 3, block, 0)
    w0, w1, w2 = (rows_ref[b, :, :n] for b in range(3))
    panel = panel_ref[...]
    l21 = gram_ref[2 * n :, :n]
    x10 = -dot_nn(w1, dot_nn(panel[:n], w0, HIGHEST), HIGHEST)
    x21 = -dot_nn(w2, dot_nn(l21, w1, HIGHEST), HIGHEST)
    x20 = -dot_nn(w2, dot_nn(panel[n:], w0, HIGHEST) + dot_nn(l21, x10, HIGHEST), HIGHEST)
    out_ref[:n, :n] = w0 * scale
    out_ref[n : 2 * n, :n] = x10 * scale
    out_ref[n : 2 * n, n : 2 * n] = w1 * scale
    out_ref[2 * n :, :n] = x20 * scale
    out_ref[2 * n :, n : 2 * n] = x21 * scale
    out_ref[2 * n :, 2 * n :] = w2 * scale


def factor_call(packed, scale):
    return pl.pallas_call(
        functools.partial(factor_body, scale=scale),
        name="factor",
        in_specs=[VMEM_SPEC],
        out_specs=VMEM_SPEC,
        scratch_shapes=[
            pltpu.VMEM((K, K), jnp.float32),
            pltpu.VMEM((4, NB, 2 * NB), jnp.float32),
            pltpu.VMEM((2 * NB, NB), jnp.float32),
        ],
        out_shape=jax.ShapeDtypeStruct((K, K), jnp.float32),
        compiler_params=pltpu.CompilerParams(vmem_limit_bytes=4 << 20),
    )(packed)


def apply_body(factor_ref, *refs):
    out_ref = refs[-1]
    both = jnp.concatenate([r[...] for r in refs[:-1]], axis=0)
    out_ref[...] = dot_nn(factor_ref[...], both, HIGHEST)


def apply_call(factor, parts):
    return pl.pallas_call(
        apply_body,
        in_specs=[VMEM_SPEC] * (1 + len(parts)),
        out_specs=VMEM_SPEC,
        out_shape=jax.ShapeDtypeStruct((K, parts[0].shape[1]), jnp.float32),
        compiler_params=pltpu.CompilerParams(vmem_limit_bytes=4 << 20),
    )(factor, *parts)


def shift(x, axis, size, by):
    return lax.ppermute(x, axis, [(i, (i + by) % size) for i in range(size)])


def reduce_z(parts):
    chains = []
    for half, part in enumerate(parts):
        up, down = (4, 3) if half == 0 else (3, 4)
        chains.append([part[up], part[NZ - down], up, down])
    for _ in range(4):
        for chain, part in zip(chains, parts):
            if chain[2]:
                chain[0] = shift(chain[0], "z", NZ, 1)
                chain[2] -= 1
                if chain[2]:
                    chain[0] = chain[0] + part[chain[2]]
            if chain[3]:
                chain[1] = shift(chain[1], "z", NZ, -1)
                chain[3] -= 1
                if chain[3]:
                    chain[1] = chain[1] + part[NZ - chain[3]]
    return [chain[0] + chain[1] + part[0] for chain, part in zip(chains, parts)]


def gather_z(own):
    found = [[mine] + [None] * (NZ - 1) for mine in own]
    for step in range(1, 5):
        for half, got in enumerate(found):
            if step <= (4 if half == 0 else 3):
                got[NZ - step] = shift(got[(NZ - step + 1) % NZ], "z", NZ, 1)
            if step <= (3 if half == 0 else 4):
                got[step] = shift(got[step - 1], "z", NZ, -1)
    return found


def shift_xy(x, by, stage):
    pairs = []
    for i in range(32):
        px, py, core = i // 8, i // 2 % 4, i % 2
        if core == stage:
            px = (px + by) % 4
        else:
            py = (py + by) % 4
        pairs.append((i, (px * 4 + py) * 2 + core))
    return lax.ppermute(x, ("x", "y", "core"), pairs)


def exchange(blocks, stage):
    total = blocks[0]
    for d in (2, 1, 3):
        total = total + shift_xy(blocks[d], d, stage)
    return total


def per_device(tiles, tile_coords, live_counts):
    x, y, core, z = (lax.axis_index(name).astype(jnp.int32) for name in ("x", "y", "core", "z"))
    pos = jnp.stack([z, core, x, y])
    slots = jnp.arange(NT, dtype=jnp.int32)
    live = slots < live_counts[0]
    relative = (tile_coords[:, 0] - 2 * z) & (RT - 1)
    meta = jnp.where(live, relative, RT) * CT + tile_coords[:, 1]
    parts = sketch_call(meta, live_counts, pos, tiles)
    far = (relative >= 2 * FAR[0]) & (relative < 2 * FAR[-1] + 2)
    key = jnp.where(live, far.astype(jnp.int32), 2) * NT + slots
    rank = jnp.sum((key[:, None] > key[None, :]).astype(jnp.int32), axis=1)
    order = jnp.sum(jnp.where(rank[:, None] == slots[None, :], slots[:, None], 0), axis=0)
    count = jnp.stack([jnp.sum(live & ~far), jnp.sum(live & far)]).astype(jnp.int32)
    own = reduce_z([parts[:NZ], parts[NZ:]])
    found = gather_z(own)
    near = [got[d] for got in found for d in NEAR]
    near_split, near_gram = split_call(near)
    carried = adjoint_call(order, meta, count, pos, tiles, near_split, NEAR)
    rest = [got[d] for got in found for d in FAR]
    far_split, gram = split_call(rest, (near_gram,))
    gram = gram + shift(gram, "core", 2, 1)
    keep, give = adjoint_call(order, meta, count, pos, tiles, far_split, FAR, carried)
    gram = exchange([gram] * 4, 0)
    blocks = (keep + shift(give, "core", 2, 1)).reshape(4, 4, K, 128)
    gram = exchange([gram] * 4, 1)
    blocks = exchange([blocks[d] for d in range(4)], 0)
    block = exchange([blocks[d] for d in range(4)], 1)
    scale = math.sqrt(RT * TB * 32)
    factor = factor_call(gram, scale)
    range_basis = apply_call(factor, own)
    projected = apply_call(factor, [block])
    return range_basis.T, projected.T[None]


def solution(mesh):
    split = Mesh(mesh.devices.reshape(4, 4, 2, NZ), ("x", "y", "core", "z"))
    row = ("x", "y", "core")
    both = (*row, "z")
    in_specs = (P(both, None, None), P(both, None), P(both))
    out_specs = (P(both, None), P("z", row, None))
    return jax.shard_map(
        per_device, mesh=split, in_specs=in_specs, out_specs=out_specs, check_vma=False
    )
```

```python
import functools
import math

import jax
import jax.numpy as jnp
from jax import lax
from jax.experimental import pallas as pl
from jax.experimental.pallas import tpu as pltpu
from jax.sharding import Mesh
from jax.sharding import PartitionSpec as P

TB = 256
K = 192
RT = 16
CT = 16
NT = 96
NZ = 8
KH = K // 2
CH = RT * TB // NZ
SLOTS = 8
UNROLL = 4
STEPS = NT // SLOTS
HIGHEST = lax.Precision.HIGHEST


def dot_nt(a, b, precision=None):
    return lax.dot_general(
        a, b, (((1,), (1,)), ((), ())), precision=precision, preferred_element_type=jnp.float32
    )


def dot_nn(a, b, precision=None):
    return lax.dot_general(
        a, b, (((1,), (0,)), ((), ())), precision=precision, preferred_element_type=jnp.float32
    )


SMEM_SPEC = pl.BlockSpec(memory_space=pltpu.SMEM)
VMEM_SPEC = pl.BlockSpec(memory_space=pltpu.VMEM)
HBM_SPEC = pl.BlockSpec(memory_space=pltpu.HBM)


def place_on_mesh(index_ref):
    index = index_ref[0]
    return (index >> 6) & 3, (index >> 4) & 3, (index >> 3) & 1, index & 7


def sketch_body(coords_ref, live_ref, index_ref, tiles_ref, *refs):
    outs = refs[: 2 * NZ]
    omega_ref, acc_ref, buf_ref, sems = refs[2 * NZ :]
    steps = (live_ref[0] + SLOTS - 1) >> 3

    def copy(step):
        return pltpu.make_async_copy(
            tiles_ref.at[pl.ds(step * SLOTS, SLOTS)],
            buf_ref.at[pl.ds(step * SLOTS, SLOTS)],
            sems.at[step],
        )

    def fetch(step, carry):
        copy(step).start()
        return carry

    lax.fori_loop(0, steps, fetch, 0)
    k_ids = lax.broadcasted_iota(jnp.int32, (K, TB), 0)
    g_ids = lax.broadcasted_iota(jnp.int32, (K, TB), 1)
    base = g_ids * K + k_ids
    z = place_on_mesh(index_ref)[3]

    def fill(j, carry):
        h = base + (z * CT + j) * (TB * K)
        h = h * 747796405 + 1442695040
        h = h ^ (h >> 15)
        h = h * 1103515245 + 12345
        h = h ^ (h >> 13)
        omega_ref[j] = (1 - 2 * ((h >> 9) & 1)).astype(jnp.float32).astype(jnp.bfloat16)
        acc_ref[j] = jnp.zeros((K, TB), jnp.float32)
        return carry

    lax.fori_loop(0, CT, fill, 0)

    def work(step, carry):
        copy(step).wait()
        for t in range(SLOTS):
            slot = step * SLOTS + t
            i = (coords_ref[0, slot] - 2 * z) & (RT - 1)
            i = jnp.where(slot < live_ref[0], i, RT)
            acc_ref[i] += dot_nt(omega_ref[coords_ref[1, slot]], buf_ref[slot])
        return carry

    lax.fori_loop(0, steps, work, 0)
    for d in range(NZ):
        for half in range(2):
            for e in range(2):
                outs[half * NZ + d][:, e * TB : (e + 1) * TB] = acc_ref[
                    2 * d + e, half * KH : (half + 1) * KH, :
                ]


def sketch_call(coords, live, index, tiles):
    return pl.pallas_call(
        sketch_body,
        name="sketch",
        in_specs=[SMEM_SPEC, SMEM_SPEC, SMEM_SPEC, HBM_SPEC],
        out_specs=[VMEM_SPEC] * (2 * NZ),
        scratch_shapes=[
            pltpu.VMEM((CT, K, TB), jnp.bfloat16),
            pltpu.VMEM((RT + 1, K, TB), jnp.float32),
            pltpu.VMEM((NT, TB, TB), jnp.bfloat16),
            pltpu.SemaphoreType.DMA((STEPS,)),
        ],
        out_shape=[jax.ShapeDtypeStruct((KH, CH), jnp.float32)] * (2 * NZ),
        compiler_params=pltpu.CompilerParams(vmem_limit_bytes=24 << 20),
    )(coords, live, index, tiles)


NEAR = (0, 1, 2, 6, 7)
FAR = (3, 4, 5)


def split_body(*refs, n, last):
    chunks = refs[: 2 * n]
    split_ref, gram_ref, sum_ref = refs[-3:]

    for c in range(n):
        for half in range(2):
            chunk = chunks[half * n + c]

            def part(g, carry):
                rows = pl.ds(pl.multiple_of(g * 32, 32), 32)
                at = pl.multiple_of(half * KH + g * 32, 32)
                full = chunk[rows, :]
                high = full.astype(jnp.bfloat16)
                low = (full - high.astype(jnp.float32)).astype(jnp.bfloat16)
                for e in range(2):
                    cols = slice(e * TB, (e + 1) * TB)
                    split_ref[2 * c + e, pl.ds(at, 32), :] = high[:, cols]
                    split_ref[2 * c + e, pl.ds(K + at, 32), :] = low[:, cols]
                return carry

            lax.fori_loop(0, KH // 32, part, 0)
    sum_ref[...] = jnp.zeros((2 * K, K), jnp.float32)

    def square(i, carry):
        sum_ref[...] += dot_nt(split_ref[i], split_ref[i, :K, :])
        return carry

    lax.fori_loop(0, 2 * n, square, 0)
    cross = sum_ref[K:, :]
    gram = sum_ref[:K, :] + (cross + cross.T)
    if last:
        gram = refs[2 * n][...] + gram
        for row, col, (i, j) in PACKED:
            gram_ref[row : row + NB, col : col + NB] = gram[i : i + NB, j : j + NB]
    else:
        gram_ref[...] = gram


NB = 64
PACKED = (
    (0, 0, (0, 0)),
    (0, NB, (NB, 0)),
    (NB, 0, (2 * NB, 0)),
    (NB, NB, (NB, NB)),
    (2 * NB, 0, (2 * NB, 2 * NB)),
    (2 * NB, NB, (2 * NB, NB)),
)


def split_call(chunks, carried=()):
    n = len(chunks) // 2
    return pl.pallas_call(
        functools.partial(split_body, n=n, last=bool(carried)),
        name="split_far" if carried else "split_near",
        in_specs=[VMEM_SPEC] * (len(chunks) + len(carried)),
        out_specs=[VMEM_SPEC] * 2,
        scratch_shapes=[pltpu.VMEM((2 * K, K), jnp.float32)],
        out_shape=[
            jax.ShapeDtypeStruct((2 * n, 2 * K, TB), jnp.bfloat16),
            jax.ShapeDtypeStruct((K, 2 * NB) if carried else (K, K), jnp.float32),
        ],
        compiler_params=pltpu.CompilerParams(vmem_limit_bytes=8 << 20),
    )(*chunks, *carried)


def adjoint_body(
    order_ref, coords_ref, count_ref, index_ref, tiles_ref, split_ref, *refs, dists, last
):
    if last:
        acc_in, keep_ref, give_ref = refs[:3]
    else:
        acc_out = refs[0]
    acc_ref, buf_ref, sems = refs[-3:]
    first = count_ref[0] if last else 0
    total = count_ref[1] if last else count_ref[0]
    steps = (total + UNROLL - 1) >> 2
    x, y, core, z = place_on_mesh(index_ref)

    def copy(step, t):
        rank = step * UNROLL + t
        slot = order_ref[jnp.minimum(first + rank, NT - 1)]
        return pltpu.make_async_copy(tiles_ref.at[slot], buf_ref.at[rank], sems.at[step])

    def fetch(step, carry):
        for t in range(UNROLL):
            copy(step, t).start()
        return carry

    lax.fori_loop(0, steps, fetch, 0)

    def clear(j, carry):
        acc_ref[j] = acc_in[j] if last else jnp.zeros((K, TB), jnp.float32)
        return carry

    lax.fori_loop(0, CT, clear, 0)

    def work(step, carry):
        for t in range(UNROLL):
            copy(step, t).wait()
        for t in range(UNROLL):
            rank = step * UNROLL + t
            slot = order_ref[jnp.minimum(first + rank, NT - 1)]
            i = place_of((coords_ref[0, slot] - 2 * z) & (RT - 1), dists)
            j = jnp.where(rank < total, coords_ref[1, slot], CT)
            part = dot_nn(split_ref[i], buf_ref[rank])
            acc_ref[j] += part[:K] + part[K:]
        return carry

    lax.fori_loop(0, steps, work, 0)
    if last:
        mine = pl.multiple_of(core * 128, 128)
        other = pl.multiple_of((1 - core) * 128, 128)

        def place(q, carry):
            one = q >> 2
            two = q & 3
            swap = core == 1
            own = chip_of(x, y, jnp.where(swap, two, one), jnp.where(swap, one, two))
            far = chip_of(x, y, jnp.where(swap, one, two), jnp.where(swap, two, one))
            keep_ref[q] = acc_ref[own, :, pl.ds(mine, 128)]
            give_ref[q] = acc_ref[far, :, pl.ds(other, 128)]
            return carry

        lax.fori_loop(0, CT, place, 0)
    else:

        def save(j, carry):
            acc_out[j] = acc_ref[j]
            return carry

        lax.fori_loop(0, CT, save, 0)


def place_of(i, dists):
    if dists == FAR:
        return jnp.clip(i - 2 * FAR[0], 0, 2 * len(FAR) - 1)
    return jnp.clip(jnp.where(i >= 12, i - 6, i), 0, 2 * len(NEAR) - 1)


def chip_of(x, y, dx, dy):
    return ((x + dx) & 3) * 4 + ((y + dy) & 3)


def adjoint_call(order, coords, count, index, tiles, split, dists, carried=()):
    last = bool(carried)
    part = (CT, K, 128)
    outs = [part, part] if last else [(CT, K, TB)]
    return pl.pallas_call(
        functools.partial(adjoint_body, dists=dists, last=last),
        name="adjoint_far" if last else "adjoint_near",
        in_specs=[SMEM_SPEC] * 4 + [HBM_SPEC] + [VMEM_SPEC] * (1 + len(carried)),
        out_specs=[VMEM_SPEC] * len(outs),
        scratch_shapes=[
            pltpu.VMEM((CT + 1, K, TB), jnp.float32),
            pltpu.VMEM((NT, TB, TB), jnp.bfloat16),
            pltpu.SemaphoreType.DMA((NT // UNROLL,)),
        ],
        out_shape=[jax.ShapeDtypeStruct(o, jnp.float32) for o in outs],
        compiler_params=pltpu.CompilerParams(vmem_limit_bytes=24 << 20),
    )(order, coords, count, index, tiles, split, *carried)


def inverse_factor(block, rows_ref):
    eye = (
        lax.broadcasted_iota(jnp.int32, (NB, NB), 0) == lax.broadcasted_iota(jnp.int32, (NB, NB), 1)
    ).astype(jnp.float32)
    work = jnp.concatenate([eye, block], axis=1)
    first = 0
    for k in range(0, NB, 2):
        o = k - first
        rows = NB - first
        a = jnp.broadcast_to(work[:, NB + k : NB + k + 1], (rows, 2 * NB))
        b = jnp.broadcast_to(work[:, NB + k + 1 : NB + k + 2], (rows, 2 * NB))
        p = a[o : o + 1]
        q = a[o + 1 : o + 2]
        r = b[o + 1 : o + 2]
        r0 = work[o : o + 1]
        r1 = work[o + 1 : o + 2]
        inv = 1.0 / (p * r - q * q)
        u0 = (r * r0 - q * r1) * inv
        u1 = (p * r1 - q * r0) * inv
        rows_ref[k : k + 1, :] = r0 * lax.rsqrt(p)
        ratio = q / p
        rows_ref[k + 1 : k + 2, :] = (r1 - ratio * r0) * lax.rsqrt(r - ratio * q)
        if k + 2 == NB:
            break
        skip = (k + 2) // 8 * 8 - first
        if skip:
            work, a, b = work[skip:], a[skip:], b[skip:]
            first += skip
        if (k + 2) % 8:
            below = lax.broadcasted_iota(jnp.int32, a.shape, 0) >= k + 2 - first
            a = jnp.where(below, a, 0.0)
            b = jnp.where(below, b, 0.0)
        work = work - (a * u0 + b * u1)
    return rows_ref[:, :NB]


def factor_body(packed_ref, out_ref, gram_ref, rows_ref, panel_ref, *, scale):
    n = NB
    for row, col, (i, j) in PACKED:
        block = packed_ref[row : row + n, col : col + n]
        gram_ref[i : i + n, j : j + n] = block
        if i == 2 * n and j == n:
            gram_ref[j : j + n, i : i + n] = block.T
    rows_ref[3, :, :n] = gram_ref[:n, :n]
    out_ref[...] = jnp.zeros((K, K), jnp.float32)

    def block(b, carry):
        w = inverse_factor(rows_ref[3, :, :n], rows_ref.at[b])

        @pl.when(b == 0)
        def _():
            panel = dot_nt(gram_ref[n:, :n], w, HIGHEST)
            panel_ref[...] = panel
            trail = gram_ref[n:, n:] - dot_nt(panel, panel, HIGHEST)
            gram_ref[n:, n:] = trail
            rows_ref[3] = trail[:n]

        @pl.when(b == 1)
        def _():
            l21 = dot_nt(gram_ref[2 * n :, n : 2 * n], w, HIGHEST)
            gram_ref[2 * n :, :n] = l21
            rows_ref[3, :, :n] = gram_ref[2 * n :, 2 * n :] - dot_nt(l21, l21, HIGHEST)

        return carry

    lax.fori_loop(0, 3, block, 0)
    w0, w1, w2 = (rows_ref[b, :, :n] for b in range(3))
    panel = panel_ref[...]
    l21 = gram_ref[2 * n :, :n]
    x10 = -dot_nn(w1, dot_nn(panel[:n], w0, HIGHEST), HIGHEST)
    x21 = -dot_nn(w2, dot_nn(l21, w1, HIGHEST), HIGHEST)
    x20 = -dot_nn(w2, dot_nn(panel[n:], w0, HIGHEST) + dot_nn(l21, x10, HIGHEST), HIGHEST)
    out_ref[:n, :n] = w0 * scale
    out_ref[n : 2 * n, :n] = x10 * scale
    out_ref[n : 2 * n, n : 2 * n] = w1 * scale
    out_ref[2 * n :, :n] = x20 * scale
    out_ref[2 * n :, n : 2 * n] = x21 * scale
    out_ref[2 * n :, 2 * n :] = w2 * scale


def factor_call(packed, scale):
    return pl.pallas_call(
        functools.partial(factor_body, scale=scale),
        name="factor",
        in_specs=[VMEM_SPEC],
        out_specs=VMEM_SPEC,
        scratch_shapes=[
            pltpu.VMEM((K, K), jnp.float32),
            pltpu.VMEM((4, NB, 2 * NB), jnp.float32),
            pltpu.VMEM((2 * NB, NB), jnp.float32),
        ],
        out_shape=jax.ShapeDtypeStruct((K, K), jnp.float32),
        compiler_params=pltpu.CompilerParams(vmem_limit_bytes=4 << 20),
    )(packed)


def apply_body(factor_ref, *refs):
    out_ref = refs[-1]
    both = jnp.concatenate([r[...] for r in refs[:-1]], axis=0)
    out_ref[...] = dot_nn(factor_ref[...], both, HIGHEST)


def apply_call(factor, parts):
    return pl.pallas_call(
        apply_body,
        in_specs=[VMEM_SPEC] * (1 + len(parts)),
        out_specs=VMEM_SPEC,
        out_shape=jax.ShapeDtypeStruct((K, parts[0].shape[1]), jnp.float32),
        compiler_params=pltpu.CompilerParams(vmem_limit_bytes=4 << 20),
    )(factor, *parts)


def shift(x, axis, size, by):
    return lax.ppermute(x, axis, [(i, (i + by) % size) for i in range(size)])


def reduce_z(parts):
    chains = []
    for half, part in enumerate(parts):
        up, down = (4, 3) if half == 0 else (3, 4)
        chains.append([part[up], part[NZ - down], up, down])
    for _ in range(4):
        for chain, part in zip(chains, parts):
            if chain[2]:
                chain[0] = shift(chain[0], "z", NZ, 1)
                chain[2] -= 1
                if chain[2]:
                    chain[0] = chain[0] + part[chain[2]]
            if chain[3]:
                chain[1] = shift(chain[1], "z", NZ, -1)
                chain[3] -= 1
                if chain[3]:
                    chain[1] = chain[1] + part[NZ - chain[3]]
    return [chain[0] + chain[1] + part[0] for chain, part in zip(chains, parts)]


def gather_z(own):
    found = [[mine] + [None] * (NZ - 1) for mine in own]
    for step in range(1, 5):
        for half, got in enumerate(found):
            if step <= (4 if half == 0 else 3):
                got[NZ - step] = shift(got[(NZ - step + 1) % NZ], "z", NZ, 1)
            if step <= (3 if half == 0 else 4):
                got[step] = shift(got[step - 1], "z", NZ, -1)
    return found


def shift_xy(x, by, stage):
    pairs = []
    for i in range(32):
        px, py, core = i // 8, i // 2 % 4, i % 2
        if core == stage:
            px = (px + by) % 4
        else:
            py = (py + by) % 4
        pairs.append((i, (px * 4 + py) * 2 + core))
    return lax.ppermute(x, ("x", "y", "core"), pairs)


def exchange(blocks, stage):
    total = blocks[0]
    for d in (2, 1, 3):
        total = total + shift_xy(blocks[d], d, stage)
    return total


def per_device(tiles, tile_coords, live_counts):
    index = lax.axis_index(("x", "y", "core", "z")).astype(jnp.int32).reshape(1)
    coords = tile_coords.T
    tiles = pltpu.with_memory_space_constraint(tiles, pltpu.HBM)
    parts = sketch_call(coords, live_counts, index, tiles)
    slots = jnp.arange(NT, dtype=jnp.int32)
    live = slots < live_counts[0]
    relative = (coords[0] - 2 * (index[0] & (NZ - 1))) & (RT - 1)
    far = (relative >= 2 * FAR[0]) & (relative < 2 * FAR[-1] + 2)
    key = jnp.where(live, far.astype(jnp.int32), 2) * NT + slots
    rank = jnp.sum((key[:, None] > key[None, :]).astype(jnp.int32), axis=1)
    order = jnp.sum(jnp.where(rank[:, None] == slots[None, :], slots[:, None], 0), axis=0)
    count = jnp.stack([jnp.sum(live & ~far), jnp.sum(live & far)]).astype(jnp.int32)
    own = reduce_z([parts[:NZ], parts[NZ:]])
    found = gather_z(own)
    near = [got[d] for got in found for d in NEAR]
    near_split, near_gram = split_call(near)
    carried = adjoint_call(order, coords, count, index, tiles, near_split, NEAR)
    rest = [got[d] for got in found for d in FAR]
    far_split, gram = split_call(rest, (near_gram,))
    gram = gram + shift(gram, "core", 2, 1)
    keep, give = adjoint_call(order, coords, count, index, tiles, far_split, FAR, carried)
    gram = exchange([gram] * 4, 0)
    blocks = (keep + shift(give, "core", 2, 1)).reshape(4, 4, K, 128)
    gram = exchange([gram] * 4, 1)
    blocks = exchange([blocks[d] for d in range(4)], 0)
    block = exchange([blocks[d] for d in range(4)], 1)
    scale = math.sqrt(RT * TB * 32)
    factor = factor_call(gram, scale)
    range_basis = apply_call(factor, own)
    projected = apply_call(factor, [block])
    return range_basis.T, projected.T[None]


def solution(mesh):
    split = Mesh(mesh.devices.reshape(4, 4, 2, NZ), ("x", "y", "core", "z"))
    row = ("x", "y", "core")
    both = (*row, "z")
    in_specs = (P(both, None, None), P(both, None), P(both))
    out_specs = (P(both, None), P("z", row, None))
    return jax.shard_map(
        per_device, mesh=split, in_specs=in_specs, out_specs=out_specs, check_vma=False
    )
```

```python
import functools
import math

import jax
import jax.numpy as jnp
from jax import lax
from jax.experimental import pallas as pl
from jax.experimental.pallas import tpu as pltpu
from jax.sharding import Mesh
from jax.sharding import PartitionSpec as P

TB = 256
K = 192
RT = 16
CT = 16
NT = 96
NZ = 8
KH = K // 2
CH = RT * TB // NZ
SLOTS = 8
UNROLL = 4
NEAR = (0, 1, 2, 6, 7)
FAR = (3, 4, 5)
STEPS = NT // SLOTS
HIGHEST = lax.Precision.HIGHEST


def dot_nt(a, b, precision=None):
    return lax.dot_general(
        a, b, (((1,), (1,)), ((), ())), precision=precision, preferred_element_type=jnp.float32
    )


def dot_nn(a, b, precision=None):
    return lax.dot_general(
        a, b, (((1,), (0,)), ((), ())), precision=precision, preferred_element_type=jnp.float32
    )


SMEM_SPEC = pl.BlockSpec(memory_space=pltpu.SMEM)
VMEM_SPEC = pl.BlockSpec(memory_space=pltpu.VMEM)
HBM_SPEC = pl.BlockSpec(memory_space=pltpu.HBM)


def place_on_mesh(index_ref):
    index = index_ref[0]
    return (index >> 6) & 3, (index >> 4) & 3, (index >> 3) & 1, index & 7


def relative_row(coords_ref, slot, z):
    return (coords_ref[0, slot] - 2 * z) & (RT - 1)


def place_of(i, dists):
    if dists == FAR:
        return jnp.clip(i - 2 * FAR[0], 0, 2 * len(FAR) - 1)
    return jnp.clip(jnp.where(i >= 12, i - 6, i), 0, 2 * len(NEAR) - 1)


def sketch_tiles(steps, total, slot_at, coords_ref, z, omega_ref, buf_ref, acc_ref, dists, ready):
    def work(step, carry):
        carry = ready(slot_at(step * UNROLL + UNROLL - 1), carry)
        for t in range(UNROLL):
            rank = step * UNROLL + t
            slot = slot_at(rank)
            i = place_of(relative_row(coords_ref, slot, z), dists)
            i = jnp.where(rank < total, i, 2 * len(dists))
            acc_ref[i] += dot_nt(omega_ref[coords_ref[1, slot]], buf_ref[slot])
        return carry

    return lax.fori_loop(0, steps, work, 0)


def store_parts(outs, acc_ref, n):
    for c in range(n):
        for half in range(2):
            for e in range(2):
                outs[half * n + c][:, e * TB : (e + 1) * TB] = acc_ref[
                    2 * c + e, half * KH : (half + 1) * KH, :
                ]


def sketch_far_body(coords_ref, live_ref, index_ref, tiles_ref, *refs):
    n = len(FAR)
    outs = refs[: 2 * n]
    omega_ref, buf_ref, near_ref, far_ref, count_ref, acc_ref, sems = refs[2 * n :]
    batches = (live_ref[0] + SLOTS - 1) >> 3
    z = place_on_mesh(index_ref)[3]

    def copy(batch):
        part = pl.ds(batch * SLOTS, SLOTS)
        return pltpu.make_async_copy(tiles_ref.at[part], buf_ref.at[part], sems.at[batch])

    def fetch(batch, carry):
        copy(batch).start()
        return carry

    def land(batch, carry):
        copy(batch).wait()
        return carry

    lax.fori_loop(0, batches, fetch, 0)
    k_ids = lax.broadcasted_iota(jnp.int32, (K, TB), 0)
    g_ids = lax.broadcasted_iota(jnp.int32, (K, TB), 1)
    base = g_ids * K + k_ids

    def fill(j, found):
        h = base + (z * CT + j) * (TB * K)
        h = h * 747796405 + 1442695040
        h = h ^ (h >> 15)
        h = h * 1103515245 + 12345
        h = h ^ (h >> 13)
        omega_ref[j] = (1 - 2 * ((h >> 9) & 1)).astype(jnp.float32).astype(jnp.bfloat16)
        near, far = found
        for t in range(NT // CT):
            slot = j * (NT // CT) + t
            i = relative_row(coords_ref, slot, z)
            inside = jnp.where((i >= 2 * FAR[0]) & (i < 2 * FAR[-1] + 2), 1, 0)
            live = jnp.where(slot < live_ref[0], 1, 0)
            far_ref[far] = slot
            near_ref[near] = slot
            far += live * inside
            near += live * (1 - inside)
        return near, far

    near, far = lax.fori_loop(0, CT, fill, (jnp.int32(0), jnp.int32(0)))
    count_ref[0] = near
    count_ref[1] = far
    acc_ref[...] = jnp.zeros(acc_ref.shape, jnp.float32)

    def slot_at(rank):
        return far_ref[jnp.minimum(rank, far - 1)]

    def ready(slot, landed):
        upto = (slot >> 3) + 1
        lax.fori_loop(landed, upto, land, 0)
        return upto

    steps = (far + UNROLL - 1) >> 2
    landed = sketch_tiles(
        steps, far, slot_at, coords_ref, z, omega_ref, buf_ref, acc_ref, FAR, ready
    )
    store_parts(outs, acc_ref, n)
    lax.fori_loop(landed, batches, land, 0)


def sketch_near_body(coords_ref, index_ref, near_ref, count_ref, omega_ref, buf_ref, *refs):
    n = len(NEAR)
    outs, acc_ref = refs[: 2 * n], refs[2 * n]
    total = count_ref[0]
    z = place_on_mesh(index_ref)[3]
    acc_ref[...] = jnp.zeros(acc_ref.shape, jnp.float32)

    def slot_at(rank):
        return near_ref[jnp.minimum(rank, total - 1)]

    steps = (total + UNROLL - 1) >> 2
    sketch_tiles(
        steps, total, slot_at, coords_ref, z, omega_ref, buf_ref, acc_ref, NEAR, lambda _, c: c
    )
    store_parts(outs, acc_ref, n)


def sketch_near_call(coords, index, near, count, omega, held, shape, limit):
    m = len(NEAR)
    return pl.pallas_call(
        sketch_near_body,
        name="sketch_near",
        in_specs=[SMEM_SPEC] * 4 + [VMEM_SPEC] * 2,
        out_specs=[VMEM_SPEC] * (2 * m),
        scratch_shapes=[pltpu.VMEM((2 * m + 1, K, TB), jnp.float32)],
        out_shape=[shape] * (2 * m),
        compiler_params=limit,
    )(coords, index, near, count, omega, held)


def sketch_calls(coords, live, index, tiles):
    shape = jax.ShapeDtypeStruct((KH, CH), jnp.float32)
    limit = pltpu.CompilerParams(vmem_limit_bytes=24 << 20)
    n = len(FAR)
    got = pl.pallas_call(
        sketch_far_body,
        name="sketch_far",
        in_specs=[SMEM_SPEC] * 3 + [HBM_SPEC],
        out_specs=[VMEM_SPEC] * (2 * n + 2) + [SMEM_SPEC] * 3,
        scratch_shapes=[
            pltpu.VMEM((2 * n + 1, K, TB), jnp.float32),
            pltpu.SemaphoreType.DMA((STEPS,)),
        ],
        out_shape=[shape] * (2 * n)
        + [
            jax.ShapeDtypeStruct((CT, K, TB), jnp.bfloat16),
            jax.ShapeDtypeStruct((NT, TB, TB), jnp.bfloat16),
            jax.ShapeDtypeStruct((NT,), jnp.int32),
            jax.ShapeDtypeStruct((NT,), jnp.int32),
            jax.ShapeDtypeStruct((2,), jnp.int32),
        ],
        compiler_params=limit,
    )(coords, live, index, tiles)
    omega, held, near, far, count = got[2 * n :]
    rest = sketch_near_call(coords, index, near, count, omega, held, shape, limit)
    m = len(NEAR)
    parts = [[None] * NZ for _ in range(2)]
    for half in range(2):
        for c, d in enumerate(FAR):
            parts[half][d] = got[half * n + c]
        for c, d in enumerate(NEAR):
            parts[half][d] = rest[half * m + c]
    return parts, held, near, far, count


def split_body(*refs, n, last):
    chunks = refs[: 2 * n]
    split_ref, gram_ref, sum_ref = refs[-3:]

    for c in range(n):
        for half in range(2):
            chunk = chunks[half * n + c]

            def part(g, carry):
                rows = pl.ds(pl.multiple_of(g * 32, 32), 32)
                at = pl.multiple_of(half * KH + g * 32, 32)
                full = chunk[rows, :]
                high = full.astype(jnp.bfloat16)
                low = (full - high.astype(jnp.float32)).astype(jnp.bfloat16)
                for e in range(2):
                    cols = slice(e * TB, (e + 1) * TB)
                    split_ref[2 * c + e, pl.ds(at, 32), :] = high[:, cols]
                    split_ref[2 * c + e, pl.ds(K + at, 32), :] = low[:, cols]
                return carry

            lax.fori_loop(0, KH // 32, part, 0)
    sum_ref[...] = jnp.zeros((2 * K, K), jnp.float32)

    def square(i, carry):
        sum_ref[...] += dot_nt(split_ref[i], split_ref[i, :K, :])
        return carry

    lax.fori_loop(0, 2 * n, square, 0)
    cross = sum_ref[K:, :]
    gram = sum_ref[:K, :] + (cross + cross.T)
    if last:
        gram = refs[2 * n][...] + gram
        for row, col, (i, j) in PACKED:
            gram_ref[row : row + NB, col : col + NB] = gram[i : i + NB, j : j + NB]
    else:
        gram_ref[...] = gram


NB = 64
PACKED = (
    (0, 0, (0, 0)),
    (0, NB, (NB, 0)),
    (NB, 0, (2 * NB, 0)),
    (NB, NB, (NB, NB)),
    (2 * NB, 0, (2 * NB, 2 * NB)),
    (2 * NB, NB, (2 * NB, NB)),
)


def split_call(chunks, carried=()):
    n = len(chunks) // 2
    return pl.pallas_call(
        functools.partial(split_body, n=n, last=bool(carried)),
        name="split_far" if carried else "split_near",
        in_specs=[VMEM_SPEC] * (len(chunks) + len(carried)),
        out_specs=[VMEM_SPEC] * 2,
        scratch_shapes=[pltpu.VMEM((2 * K, K), jnp.float32)],
        out_shape=[
            jax.ShapeDtypeStruct((2 * n, 2 * K, TB), jnp.bfloat16),
            jax.ShapeDtypeStruct((K, 2 * NB) if carried else (K, K), jnp.float32),
        ],
        compiler_params=pltpu.CompilerParams(vmem_limit_bytes=8 << 20),
    )(*chunks, *carried)


def adjoint_body(
    list_ref, coords_ref, count_ref, index_ref, buf_ref, split_ref, *refs, dists, last
):
    if last:
        acc_in, keep_ref, give_ref = refs[:3]
    else:
        acc_out = refs[0]
    acc_ref = refs[-1]
    total = count_ref[1] if last else count_ref[0]
    steps = (total + UNROLL - 1) >> 2
    x, y, core, z = place_on_mesh(index_ref)

    def clear(j, carry):
        acc_ref[j] = acc_in[j] if last else jnp.zeros((K, TB), jnp.float32)
        return carry

    lax.fori_loop(0, CT, clear, 0)

    def work(step, carry):
        for t in range(UNROLL):
            rank = step * UNROLL + t
            slot = list_ref[jnp.minimum(rank, total - 1)]
            i = place_of(relative_row(coords_ref, slot, z), dists)
            j = jnp.where(rank < total, coords_ref[1, slot], CT)
            part = dot_nn(split_ref[i], buf_ref[slot])
            acc_ref[j] += part[:K] + part[K:]
        return carry

    lax.fori_loop(0, steps, work, 0)
    if last:
        mine = pl.multiple_of(core * 128, 128)
        other = pl.multiple_of((1 - core) * 128, 128)

        def place(q, carry):
            one = q >> 2
            two = q & 3
            swap = core == 1
            own = chip_of(x, y, jnp.where(swap, two, one), jnp.where(swap, one, two))
            far = chip_of(x, y, jnp.where(swap, one, two), jnp.where(swap, two, one))
            keep_ref[q] = acc_ref[own, :, pl.ds(mine, 128)]
            give_ref[q] = acc_ref[far, :, pl.ds(other, 128)]
            return carry

        lax.fori_loop(0, CT, place, 0)
    else:

        def save(j, carry):
            acc_out[j] = acc_ref[j]
            return carry

        lax.fori_loop(0, CT, save, 0)


def chip_of(x, y, dx, dy):
    return ((x + dx) & 3) * 4 + ((y + dy) & 3)


def adjoint_call(slots, coords, count, index, held, split, dists, carried=()):
    last = bool(carried)
    part = (CT, K, 128)
    outs = [part, part] if last else [(CT, K, TB)]
    return pl.pallas_call(
        functools.partial(adjoint_body, dists=dists, last=last),
        name="adjoint_far" if last else "adjoint_near",
        in_specs=[SMEM_SPEC] * 4 + [VMEM_SPEC] * (2 + len(carried)),
        out_specs=[VMEM_SPEC] * len(outs),
        scratch_shapes=[pltpu.VMEM((CT + 1, K, TB), jnp.float32)],
        out_shape=[jax.ShapeDtypeStruct(o, jnp.float32) for o in outs],
        compiler_params=pltpu.CompilerParams(vmem_limit_bytes=8 << 20),
    )(slots, coords, count, index, held, split, *carried)


def inverse_factor(block, rows_ref):
    eye = (
        lax.broadcasted_iota(jnp.int32, (NB, NB), 0) == lax.broadcasted_iota(jnp.int32, (NB, NB), 1)
    ).astype(jnp.float32)
    work = jnp.concatenate([eye, block], axis=1)
    first = 0
    for k in range(0, NB, 2):
        o = k - first
        rows = NB - first
        a = jnp.broadcast_to(work[:, NB + k : NB + k + 1], (rows, 2 * NB))
        b = jnp.broadcast_to(work[:, NB + k + 1 : NB + k + 2], (rows, 2 * NB))
        p = a[o : o + 1]
        q = a[o + 1 : o + 2]
        r = b[o + 1 : o + 2]
        r0 = work[o : o + 1]
        r1 = work[o + 1 : o + 2]
        inv = 1.0 / (p * r - q * q)
        u0 = (r * r0 - q * r1) * inv
        u1 = (p * r1 - q * r0) * inv
        rows_ref[k : k + 1, :] = r0 * lax.rsqrt(p)
        ratio = q / p
        rows_ref[k + 1 : k + 2, :] = (r1 - ratio * r0) * lax.rsqrt(r - ratio * q)
        if k + 2 == NB:
            break
        skip = (k + 2) // 8 * 8 - first
        if skip:
            work, a, b = work[skip:], a[skip:], b[skip:]
            first += skip
        if (k + 2) % 8:
            below = lax.broadcasted_iota(jnp.int32, a.shape, 0) >= k + 2 - first
            a = jnp.where(below, a, 0.0)
            b = jnp.where(below, b, 0.0)
        work = work - (a * u0 + b * u1)
    return rows_ref[:, :NB]


def factor_body(packed_ref, out_ref, gram_ref, rows_ref, panel_ref, *, scale):
    n = NB
    for row, col, (i, j) in PACKED:
        block = packed_ref[row : row + n, col : col + n]
        gram_ref[i : i + n, j : j + n] = block
        if i == 2 * n and j == n:
            gram_ref[j : j + n, i : i + n] = block.T
    rows_ref[3, :, :n] = gram_ref[:n, :n]
    out_ref[...] = jnp.zeros((K, K), jnp.float32)

    def block(b, carry):
        w = inverse_factor(rows_ref[3, :, :n], rows_ref.at[b])

        @pl.when(b == 0)
        def _():
            panel = dot_nt(gram_ref[n:, :n], w, HIGHEST)
            panel_ref[...] = panel
            trail = gram_ref[n:, n:] - dot_nt(panel, panel, HIGHEST)
            gram_ref[n:, n:] = trail
            rows_ref[3] = trail[:n]

        @pl.when(b == 1)
        def _():
            l21 = dot_nt(gram_ref[2 * n :, n : 2 * n], w, HIGHEST)
            gram_ref[2 * n :, :n] = l21
            rows_ref[3, :, :n] = gram_ref[2 * n :, 2 * n :] - dot_nt(l21, l21, HIGHEST)

        return carry

    lax.fori_loop(0, 3, block, 0)
    w0, w1, w2 = (rows_ref[b, :, :n] for b in range(3))
    panel = panel_ref[...]
    l21 = gram_ref[2 * n :, :n]
    x10 = -dot_nn(w1, dot_nn(panel[:n], w0, HIGHEST), HIGHEST)
    x21 = -dot_nn(w2, dot_nn(l21, w1, HIGHEST), HIGHEST)
    x20 = -dot_nn(w2, dot_nn(panel[n:], w0, HIGHEST) + dot_nn(l21, x10, HIGHEST), HIGHEST)
    out_ref[:n, :n] = w0 * scale
    out_ref[n : 2 * n, :n] = x10 * scale
    out_ref[n : 2 * n, n : 2 * n] = w1 * scale
    out_ref[2 * n :, :n] = x20 * scale
    out_ref[2 * n :, n : 2 * n] = x21 * scale
    out_ref[2 * n :, 2 * n :] = w2 * scale


def factor_call(packed, scale):
    return pl.pallas_call(
        functools.partial(factor_body, scale=scale),
        name="factor",
        in_specs=[VMEM_SPEC],
        out_specs=VMEM_SPEC,
        scratch_shapes=[
            pltpu.VMEM((K, K), jnp.float32),
            pltpu.VMEM((4, NB, 2 * NB), jnp.float32),
            pltpu.VMEM((2 * NB, NB), jnp.float32),
        ],
        out_shape=jax.ShapeDtypeStruct((K, K), jnp.float32),
        compiler_params=pltpu.CompilerParams(vmem_limit_bytes=4 << 20),
    )(packed)


def apply_body(factor_ref, *refs):
    out_ref = refs[-1]
    both = jnp.concatenate([r[...] for r in refs[:-1]], axis=0)
    out_ref[...] = dot_nn(factor_ref[...], both, HIGHEST)


def apply_call(factor, parts):
    return pl.pallas_call(
        apply_body,
        in_specs=[VMEM_SPEC] * (1 + len(parts)),
        out_specs=VMEM_SPEC,
        out_shape=jax.ShapeDtypeStruct((K, parts[0].shape[1]), jnp.float32),
        compiler_params=pltpu.CompilerParams(vmem_limit_bytes=4 << 20),
    )(factor, *parts)


def shift(x, axis, size, by):
    return lax.ppermute(x, axis, [(i, (i + by) % size) for i in range(size)])


def reduce_z(parts):
    chains = []
    for half, part in enumerate(parts):
        up, down = (4, 3) if half == 0 else (3, 4)
        chains.append([part[up], part[NZ - down], up, down])
    for _ in range(1, 5):
        for chain, part in zip(chains, parts):
            if chain[2]:
                chain[0] = shift(chain[0], "z", NZ, 1)
                chain[2] -= 1
                if chain[2]:
                    chain[0] = chain[0] + part[chain[2]]
            if chain[3]:
                chain[1] = shift(chain[1], "z", NZ, -1)
                chain[3] -= 1
                if chain[3]:
                    chain[1] = chain[1] + part[NZ - chain[3]]
    return [chain[0] + chain[1] + part[0] for chain, part in zip(chains, parts)]


def gather_z(own):
    found = [[mine] + [None] * (NZ - 1) for mine in own]
    for step in range(1, 5):
        for half, got in enumerate(found):
            if step <= (4 if half == 0 else 3):
                got[NZ - step] = shift(got[(NZ - step + 1) % NZ], "z", NZ, 1)
            if step <= (3 if half == 0 else 4):
                got[step] = shift(got[step - 1], "z", NZ, -1)
    return found


def shift_xy(x, by, stage):
    pairs = []
    for i in range(32):
        px, py, core = i // 8, i // 2 % 4, i % 2
        if core == stage:
            px = (px + by) % 4
        else:
            py = (py + by) % 4
        pairs.append((i, (px * 4 + py) * 2 + core))
    return lax.ppermute(x, ("x", "y", "core"), pairs)


def exchange(blocks, stage):
    total = blocks[0]
    for d in (2, 1, 3):
        total = total + shift_xy(blocks[d], d, stage)
    return total


def per_device(tiles, tile_coords, live_counts):
    index = lax.axis_index(("x", "y", "core", "z")).astype(jnp.int32).reshape(1)
    coords = tile_coords.T
    tiles = pltpu.with_memory_space_constraint(tiles, pltpu.HBM)
    parts, held, near_slots, far_slots, count = sketch_calls(coords, live_counts, index, tiles)
    own = reduce_z(parts)
    found = gather_z(own)
    near = [got[d] for got in found for d in NEAR]
    near_split, near_gram = split_call(near)
    carried = adjoint_call(near_slots, coords, count, index, held, near_split, NEAR)
    rest = [got[d] for got in found for d in FAR]
    far_split, gram = split_call(rest, (near_gram,))
    gram = gram + shift(gram, "core", 2, 1)
    keep, give = adjoint_call(
        far_slots, coords, count, index, held, far_split, FAR, carried
    )
    gram = exchange([gram] * 4, 0)
    blocks = (keep + shift(give, "core", 2, 1)).reshape(4, 4, K, 128)
    gram = exchange([gram] * 4, 1)
    blocks = exchange([blocks[d] for d in range(4)], 0)
    block = exchange([blocks[d] for d in range(4)], 1)
    scale = math.sqrt(RT * TB * 32)
    factor = factor_call(gram, scale)
    range_basis = apply_call(factor, own)
    projected = apply_call(factor, [block])
    return range_basis.T, projected.T[None]


def solution(mesh):
    split = Mesh(mesh.devices.reshape(4, 4, 2, NZ), ("x", "y", "core", "z"))
    row = ("x", "y", "core")
    both = (*row, "z")
    in_specs = (P(both, None, None), P(both, None), P(both))
    out_specs = (P(both, None), P("z", row, None))
    return jax.shard_map(
        per_device, mesh=split, in_specs=in_specs, out_specs=out_specs, check_vma=False
    )
```

```python
import functools
import math

import jax
import jax.numpy as jnp
from jax import lax
from jax.experimental import pallas as pl
from jax.experimental.pallas import tpu as pltpu
from jax.sharding import Mesh
from jax.sharding import PartitionSpec as P

TB = 256
K = 192
RT = 16
CT = 16
NT = 96
NZ = 8
KH = K // 2
CH = RT * TB // NZ
SLOTS = 8
UNROLL = 4
NEAR = (0, 1, 2, 6, 7)
FAR = (3, 4, 5)
STEPS = NT // SLOTS
HIGHEST = lax.Precision.HIGHEST


def dot_nt(a, b, precision=None):
    return lax.dot_general(
        a, b, (((1,), (1,)), ((), ())), precision=precision, preferred_element_type=jnp.float32
    )


def dot_nn(a, b, precision=None):
    return lax.dot_general(
        a, b, (((1,), (0,)), ((), ())), precision=precision, preferred_element_type=jnp.float32
    )


SMEM_SPEC = pl.BlockSpec(memory_space=pltpu.SMEM)
VMEM_SPEC = pl.BlockSpec(memory_space=pltpu.VMEM)
HBM_SPEC = pl.BlockSpec(memory_space=pltpu.HBM)


def place_on_mesh(index_ref):
    index = index_ref[0]
    return (index >> 6) & 3, (index >> 4) & 3, (index >> 3) & 1, index & 7


def relative_row(coords_ref, slot, z):
    return (coords_ref[0, slot] - 2 * z) & (RT - 1)


def place_of(i, dists):
    if dists == FAR:
        return jnp.clip(i - 2 * FAR[0], 0, 2 * len(FAR) - 1)
    return jnp.clip(jnp.where(i >= 12, i - 6, i), 0, 2 * len(NEAR) - 1)


AHEAD = 6


def sketch_body(coords_ref, live_ref, index_ref, tiles_ref, *refs):
    outs = refs[: 2 * NZ]
    buf_ref, near_ref, far_ref, count_ref, omega_ref, acc_ref, sems = refs[2 * NZ :]
    batches = (live_ref[0] + SLOTS - 1) >> 3
    z = place_on_mesh(index_ref)[3]

    def copy(batch):
        part = pl.ds(batch * SLOTS, SLOTS)
        return pltpu.make_async_copy(tiles_ref.at[part], buf_ref.at[part], sems.at[batch])

    def fetch(batch, carry):
        copy(batch).start()
        return carry

    lax.fori_loop(0, jnp.minimum(batches, AHEAD), fetch, 0)
    k_ids = lax.broadcasted_iota(jnp.int32, (K, TB), 0)
    g_ids = lax.broadcasted_iota(jnp.int32, (K, TB), 1)
    base = g_ids * K + k_ids

    def fill(j, found):
        h = base + (z * CT + j) * (TB * K)
        h = h * 747796405 + 1442695040
        h = h ^ (h >> 15)
        h = h * 1103515245 + 12345
        h = h ^ (h >> 13)
        omega_ref[j] = (1 - 2 * ((h >> 9) & 1)).astype(jnp.float32).astype(jnp.bfloat16)
        acc_ref[j] = jnp.zeros((K, TB), jnp.float32)
        near, far = found
        for t in range(NT // CT):
            slot = j * (NT // CT) + t
            i = relative_row(coords_ref, slot, z)
            inside = jnp.where((i >= 2 * FAR[0]) & (i < 2 * FAR[-1] + 2), 1, 0)
            live = jnp.where(slot < live_ref[0], 1, 0)
            far_ref[far] = slot
            near_ref[near] = slot
            far += live * inside
            near += live * (1 - inside)
        return near, far

    near, far = lax.fori_loop(0, CT, fill, (jnp.int32(0), jnp.int32(0)))
    count_ref[0] = near
    count_ref[1] = far

    def work(batch, carry):
        @pl.when(batch + AHEAD < batches)
        def _():
            copy(batch + AHEAD).start()

        copy(batch).wait()
        for t in range(SLOTS):
            slot = batch * SLOTS + t
            i = jnp.where(slot < live_ref[0], relative_row(coords_ref, slot, z), RT)
            acc_ref[i] += dot_nt(omega_ref[coords_ref[1, slot]], buf_ref[slot])
        return carry

    lax.fori_loop(0, batches, work, 0)
    for d in range(NZ):
        for half in range(2):
            for e in range(2):
                outs[half * NZ + d][:, e * TB : (e + 1) * TB] = acc_ref[
                    2 * d + e, half * KH : (half + 1) * KH, :
                ]


def sketch_call(coords, live, index, tiles):
    got = pl.pallas_call(
        sketch_body,
        name="sketch",
        in_specs=[SMEM_SPEC] * 3 + [HBM_SPEC],
        out_specs=[VMEM_SPEC] * (2 * NZ + 1) + [SMEM_SPEC] * 3,
        scratch_shapes=[
            pltpu.VMEM((CT, K, TB), jnp.bfloat16),
            pltpu.VMEM((RT + 1, K, TB), jnp.float32),
            pltpu.SemaphoreType.DMA((STEPS,)),
        ],
        out_shape=[jax.ShapeDtypeStruct((KH, CH), jnp.float32)] * (2 * NZ)
        + [
            jax.ShapeDtypeStruct((NT, TB, TB), jnp.bfloat16),
            jax.ShapeDtypeStruct((NT,), jnp.int32),
            jax.ShapeDtypeStruct((NT,), jnp.int32),
            jax.ShapeDtypeStruct((2,), jnp.int32),
        ],
        compiler_params=pltpu.CompilerParams(vmem_limit_bytes=24 << 20),
    )(coords, live, index, tiles)
    return [got[:NZ], got[NZ : 2 * NZ]], *got[2 * NZ :]


def split_body(*refs, n, last):
    chunks = refs[: 2 * n]
    split_ref, gram_ref, sum_ref = refs[-3:]

    for c in range(n):
        for half in range(2):
            chunk = chunks[half * n + c]

            def part(g, carry):
                rows = pl.ds(pl.multiple_of(g * 32, 32), 32)
                at = pl.multiple_of(half * KH + g * 32, 32)
                full = chunk[rows, :]
                high = full.astype(jnp.bfloat16)
                low = (full - high.astype(jnp.float32)).astype(jnp.bfloat16)
                for e in range(2):
                    cols = slice(e * TB, (e + 1) * TB)
                    split_ref[2 * c + e, pl.ds(at, 32), :] = high[:, cols]
                    split_ref[2 * c + e, pl.ds(K + at, 32), :] = low[:, cols]
                return carry

            lax.fori_loop(0, KH // 32, part, 0)
    sum_ref[...] = jnp.zeros((2 * K, K), jnp.float32)

    def square(i, carry):
        sum_ref[...] += dot_nt(split_ref[i], split_ref[i, :K, :])
        return carry

    lax.fori_loop(0, 2 * n, square, 0)
    cross = sum_ref[K:, :]
    gram = sum_ref[:K, :] + (cross + cross.T)
    if last:
        gram = refs[2 * n][...] + gram
        for row, col, (i, j) in PACKED:
            gram_ref[row : row + NB, col : col + NB] = gram[i : i + NB, j : j + NB]
    else:
        gram_ref[...] = gram


NB = 64
PACKED = (
    (0, 0, (0, 0)),
    (0, NB, (NB, 0)),
    (NB, 0, (2 * NB, 0)),
    (NB, NB, (NB, NB)),
    (2 * NB, 0, (2 * NB, 2 * NB)),
    (2 * NB, NB, (2 * NB, NB)),
)


def split_call(chunks, carried=()):
    n = len(chunks) // 2
    return pl.pallas_call(
        functools.partial(split_body, n=n, last=bool(carried)),
        name="split_far" if carried else "split_near",
        in_specs=[VMEM_SPEC] * (len(chunks) + len(carried)),
        out_specs=[VMEM_SPEC] * 2,
        scratch_shapes=[pltpu.VMEM((2 * K, K), jnp.float32)],
        out_shape=[
            jax.ShapeDtypeStruct((2 * n, 2 * K, TB), jnp.bfloat16),
            jax.ShapeDtypeStruct((K, 2 * NB) if carried else (K, K), jnp.float32),
        ],
        compiler_params=pltpu.CompilerParams(vmem_limit_bytes=8 << 20),
    )(*chunks, *carried)


def adjoint_body(
    list_ref, coords_ref, count_ref, index_ref, buf_ref, split_ref, *refs, dists, last
):
    if last:
        acc_in, keep_ref, give_ref = refs[:3]
    else:
        acc_out = refs[0]
    acc_ref = refs[-1]
    total = count_ref[1] if last else count_ref[0]
    steps = (total + UNROLL - 1) >> 2
    x, y, core, z = place_on_mesh(index_ref)

    def clear(j, carry):
        acc_ref[j] = acc_in[j] if last else jnp.zeros((K, TB), jnp.float32)
        return carry

    lax.fori_loop(0, CT, clear, 0)

    def work(step, carry):
        for t in range(UNROLL):
            rank = step * UNROLL + t
            slot = list_ref[jnp.minimum(rank, total - 1)]
            i = place_of(relative_row(coords_ref, slot, z), dists)
            j = jnp.where(rank < total, coords_ref[1, slot], CT)
            part = dot_nn(split_ref[i], buf_ref[slot])
            acc_ref[j] += part[:K] + part[K:]
        return carry

    lax.fori_loop(0, steps, work, 0)
    if last:
        mine = pl.multiple_of(core * 128, 128)
        other = pl.multiple_of((1 - core) * 128, 128)

        def place(q, carry):
            one = q >> 2
            two = q & 3
            swap = core == 1
            own = chip_of(x, y, jnp.where(swap, two, one), jnp.where(swap, one, two))
            far = chip_of(x, y, jnp.where(swap, one, two), jnp.where(swap, two, one))
            keep_ref[q] = acc_ref[own, :, pl.ds(mine, 128)]
            give_ref[q] = acc_ref[far, :, pl.ds(other, 128)]
            return carry

        lax.fori_loop(0, CT, place, 0)
    else:

        def save(j, carry):
            acc_out[j] = acc_ref[j]
            return carry

        lax.fori_loop(0, CT, save, 0)


def chip_of(x, y, dx, dy):
    return ((x + dx) & 3) * 4 + ((y + dy) & 3)


def adjoint_call(slots, coords, count, index, held, split, dists, carried=()):
    last = bool(carried)
    part = (CT, K, 128)
    outs = [part, part] if last else [(CT, K, TB)]
    return pl.pallas_call(
        functools.partial(adjoint_body, dists=dists, last=last),
        name="adjoint_far" if last else "adjoint_near",
        in_specs=[SMEM_SPEC] * 4 + [VMEM_SPEC] * (2 + len(carried)),
        out_specs=[VMEM_SPEC] * len(outs),
        scratch_shapes=[pltpu.VMEM((CT + 1, K, TB), jnp.float32)],
        out_shape=[jax.ShapeDtypeStruct(o, jnp.float32) for o in outs],
        compiler_params=pltpu.CompilerParams(vmem_limit_bytes=8 << 20),
    )(slots, coords, count, index, held, split, *carried)


def inverse_factor(block, rows_ref):
    eye = (
        lax.broadcasted_iota(jnp.int32, (NB, NB), 0) == lax.broadcasted_iota(jnp.int32, (NB, NB), 1)
    ).astype(jnp.float32)
    work = jnp.concatenate([eye, block], axis=1)
    first = 0
    for k in range(0, NB, 2):
        o = k - first
        rows = NB - first
        a = jnp.broadcast_to(work[:, NB + k : NB + k + 1], (rows, 2 * NB))
        b = jnp.broadcast_to(work[:, NB + k + 1 : NB + k + 2], (rows, 2 * NB))
        p = a[o : o + 1]
        q = a[o + 1 : o + 2]
        r = b[o + 1 : o + 2]
        r0 = work[o : o + 1]
        r1 = work[o + 1 : o + 2]
        inv = 1.0 / (p * r - q * q)
        u0 = (r * r0 - q * r1) * inv
        u1 = (p * r1 - q * r0) * inv
        rows_ref[k : k + 1, :] = r0 * lax.rsqrt(p)
        ratio = q / p
        rows_ref[k + 1 : k + 2, :] = (r1 - ratio * r0) * lax.rsqrt(r - ratio * q)
        if k + 2 == NB:
            break
        skip = (k + 2) // 8 * 8 - first
        if skip:
            work, a, b = work[skip:], a[skip:], b[skip:]
            first += skip
        if (k + 2) % 8:
            below = lax.broadcasted_iota(jnp.int32, a.shape, 0) >= k + 2 - first
            a = jnp.where(below, a, 0.0)
            b = jnp.where(below, b, 0.0)
        work = work - (a * u0 + b * u1)
    return rows_ref[:, :NB]


def factor_body(packed_ref, out_ref, gram_ref, rows_ref, panel_ref, *, scale):
    n = NB
    for row, col, (i, j) in PACKED:
        block = packed_ref[row : row + n, col : col + n]
        gram_ref[i : i + n, j : j + n] = block
        if i == 2 * n and j == n:
            gram_ref[j : j + n, i : i + n] = block.T
    rows_ref[3, :, :n] = gram_ref[:n, :n]
    out_ref[...] = jnp.zeros((K, K), jnp.float32)

    def block(b, carry):
        w = inverse_factor(rows_ref[3, :, :n], rows_ref.at[b])

        @pl.when(b == 0)
        def _():
            panel = dot_nt(gram_ref[n:, :n], w, HIGHEST)
            panel_ref[...] = panel
            trail = gram_ref[n:, n:] - dot_nt(panel, panel, HIGHEST)
            gram_ref[n:, n:] = trail
            rows_ref[3] = trail[:n]

        @pl.when(b == 1)
        def _():
            l21 = dot_nt(gram_ref[2 * n :, n : 2 * n], w, HIGHEST)
            gram_ref[2 * n :, :n] = l21
            rows_ref[3, :, :n] = gram_ref[2 * n :, 2 * n :] - dot_nt(l21, l21, HIGHEST)

        return carry

    lax.fori_loop(0, 3, block, 0)
    w0, w1, w2 = (rows_ref[b, :, :n] for b in range(3))
    panel = panel_ref[...]
    l21 = gram_ref[2 * n :, :n]
    x10 = -dot_nn(w1, dot_nn(panel[:n], w0, HIGHEST), HIGHEST)
    x21 = -dot_nn(w2, dot_nn(l21, w1, HIGHEST), HIGHEST)
    x20 = -dot_nn(w2, dot_nn(panel[n:], w0, HIGHEST) + dot_nn(l21, x10, HIGHEST), HIGHEST)
    out_ref[:n, :n] = w0 * scale
    out_ref[n : 2 * n, :n] = x10 * scale
    out_ref[n : 2 * n, n : 2 * n] = w1 * scale
    out_ref[2 * n :, :n] = x20 * scale
    out_ref[2 * n :, n : 2 * n] = x21 * scale
    out_ref[2 * n :, 2 * n :] = w2 * scale


def factor_call(packed, scale):
    return pl.pallas_call(
        functools.partial(factor_body, scale=scale),
        name="factor",
        in_specs=[VMEM_SPEC],
        out_specs=VMEM_SPEC,
        scratch_shapes=[
            pltpu.VMEM((K, K), jnp.float32),
            pltpu.VMEM((4, NB, 2 * NB), jnp.float32),
            pltpu.VMEM((2 * NB, NB), jnp.float32),
        ],
        out_shape=jax.ShapeDtypeStruct((K, K), jnp.float32),
        compiler_params=pltpu.CompilerParams(vmem_limit_bytes=4 << 20),
    )(packed)


def apply_body(factor_ref, *refs):
    out_ref = refs[-1]
    both = jnp.concatenate([r[...] for r in refs[:-1]], axis=0)
    out_ref[...] = dot_nn(factor_ref[...], both, HIGHEST)


def apply_call(factor, parts):
    return pl.pallas_call(
        apply_body,
        in_specs=[VMEM_SPEC] * (1 + len(parts)),
        out_specs=VMEM_SPEC,
        out_shape=jax.ShapeDtypeStruct((K, parts[0].shape[1]), jnp.float32),
        compiler_params=pltpu.CompilerParams(vmem_limit_bytes=4 << 20),
    )(factor, *parts)


def shift(x, axis, size, by):
    return lax.ppermute(x, axis, [(i, (i + by) % size) for i in range(size)])


def reduce_z(parts):
    chains = []
    for half, part in enumerate(parts):
        up, down = (4, 3) if half == 0 else (3, 4)
        chains.append([part[up], part[NZ - down], up, down])
    for _ in range(1, 5):
        for chain, part in zip(chains, parts):
            if chain[2]:
                chain[0] = shift(chain[0], "z", NZ, 1)
                chain[2] -= 1
                if chain[2]:
                    chain[0] = chain[0] + part[chain[2]]
            if chain[3]:
                chain[1] = shift(chain[1], "z", NZ, -1)
                chain[3] -= 1
                if chain[3]:
                    chain[1] = chain[1] + part[NZ - chain[3]]
    return [chain[0] + chain[1] + part[0] for chain, part in zip(chains, parts)]


def gather_z(own):
    found = [[mine] + [None] * (NZ - 1) for mine in own]
    for step in range(1, 5):
        for half, got in enumerate(found):
            if step <= (4 if half == 0 else 3):
                got[NZ - step] = shift(got[(NZ - step + 1) % NZ], "z", NZ, 1)
            if step <= (3 if half == 0 else 4):
                got[step] = shift(got[step - 1], "z", NZ, -1)
    return found


def shift_xy(x, by, stage):
    pairs = []
    for i in range(32):
        px, py, core = i // 8, i // 2 % 4, i % 2
        if core == stage:
            px = (px + by) % 4
        else:
            py = (py + by) % 4
        pairs.append((i, (px * 4 + py) * 2 + core))
    return lax.ppermute(x, ("x", "y", "core"), pairs)


def exchange(blocks, stage):
    total = blocks[0]
    for d in (2, 1, 3):
        total = total + shift_xy(blocks[d], d, stage)
    return total


def per_device(tiles, tile_coords, live_counts):
    index = lax.axis_index(("x", "y", "core", "z")).astype(jnp.int32).reshape(1)
    coords = tile_coords.T
    tiles = pltpu.with_memory_space_constraint(tiles, pltpu.HBM)
    parts, held, near_slots, far_slots, count = sketch_call(coords, live_counts, index, tiles)
    own = reduce_z(parts)
    found = gather_z(own)
    near = [got[d] for got in found for d in NEAR]
    near_split, near_gram = split_call(near)
    carried = adjoint_call(near_slots, coords, count, index, held, near_split, NEAR)
    rest = [got[d] for got in found for d in FAR]
    far_split, gram = split_call(rest, (near_gram,))
    gram = gram + shift(gram, "core", 2, 1)
    keep, give = adjoint_call(
        far_slots, coords, count, index, held, far_split, FAR, carried
    )
    gram = exchange([gram] * 4, 0)
    blocks = (keep + shift(give, "core", 2, 1)).reshape(4, 4, K, 128)
    gram = exchange([gram] * 4, 1)
    blocks = exchange([blocks[d] for d in range(4)], 0)
    block = exchange([blocks[d] for d in range(4)], 1)
    scale = math.sqrt(RT * TB * 32)
    factor = factor_call(gram, scale)
    range_basis = apply_call(factor, own)
    projected = apply_call(factor, [block])
    return range_basis.T, projected.T[None]


def solution(mesh):
    split = Mesh(mesh.devices.reshape(4, 4, 2, NZ), ("x", "y", "core", "z"))
    row = ("x", "y", "core")
    both = (*row, "z")
    in_specs = (P(both, None, None), P(both, None), P(both))
    out_specs = (P(both, None), P("z", row, None))
    return jax.shard_map(
        per_device, mesh=split, in_specs=in_specs, out_specs=out_specs, check_vma=False
    )
```

```python
import functools
import math

import jax
import jax.numpy as jnp
from jax import lax
from jax.experimental import pallas as pl
from jax.experimental.pallas import tpu as pltpu
from jax.sharding import Mesh
from jax.sharding import PartitionSpec as P

TB = 256
K = 192
RT = 16
CT = 16
NT = 96
NZ = 8
KH = K // 2
CH = RT * TB // NZ
SLOTS = 8
UNROLL = 4
NEAR = (0, 1, 2, 6, 7)
FAR = (3, 4, 5)
STEPS = NT // SLOTS
HIGHEST = lax.Precision.HIGHEST


def dot_nt(a, b, precision=None):
    return lax.dot_general(
        a, b, (((1,), (1,)), ((), ())), precision=precision, preferred_element_type=jnp.float32
    )


def dot_nn(a, b, precision=None):
    return lax.dot_general(
        a, b, (((1,), (0,)), ((), ())), precision=precision, preferred_element_type=jnp.float32
    )


SMEM_SPEC = pl.BlockSpec(memory_space=pltpu.SMEM)
VMEM_SPEC = pl.BlockSpec(memory_space=pltpu.VMEM)
HBM_SPEC = pl.BlockSpec(memory_space=pltpu.HBM)


def place_on_mesh(index_ref):
    index = index_ref[0]
    return (index >> 6) & 3, (index >> 4) & 3, (index >> 3) & 1, index & 7


def relative_row(coords_ref, slot, z):
    return (coords_ref[0, slot] - 2 * z) & (RT - 1)


def place_of(i, dists):
    if dists == FAR:
        return jnp.clip(i - 2 * FAR[0], 0, 2 * len(FAR) - 1)
    return jnp.clip(jnp.where(i >= 12, i - 6, i), 0, 2 * len(NEAR) - 1)


def sketch_body(coords_ref, live_ref, index_ref, tiles_ref, *refs):
    outs = refs[: 2 * NZ]
    buf_ref, omega_ref, acc_ref, sems = refs[2 * NZ :]
    batches = (live_ref[0] + SLOTS - 1) >> 3
    z = place_on_mesh(index_ref)[3]

    def copy(batch):
        part = pl.ds(batch * SLOTS, SLOTS)
        return pltpu.make_async_copy(tiles_ref.at[part], buf_ref.at[part], sems.at[batch])

    def fetch(batch, carry):
        copy(batch).start()
        return carry

    lax.fori_loop(0, batches, fetch, 0)
    k_ids = lax.broadcasted_iota(jnp.int32, (K, TB), 0)
    g_ids = lax.broadcasted_iota(jnp.int32, (K, TB), 1)
    base = g_ids * K + k_ids

    def fill(j, carry):
        h = base + (z * CT + j) * (TB * K)
        h = h * 747796405 + 1442695040
        h = h ^ (h >> 15)
        h = h * 1103515245 + 12345
        h = h ^ (h >> 13)
        omega_ref[j] = (1 - 2 * ((h >> 9) & 1)).astype(jnp.float32).astype(jnp.bfloat16)
        acc_ref[j] = jnp.zeros((K, TB), jnp.float32)
        return carry

    lax.fori_loop(0, CT, fill, 0)

    def work(batch, carry):
        copy(batch).wait()
        for t in range(SLOTS):
            slot = batch * SLOTS + t
            i = jnp.where(slot < live_ref[0], coords_ref[0, slot], RT)
            acc_ref[i] += dot_nt(omega_ref[coords_ref[1, slot]], buf_ref[slot])
        return carry

    lax.fori_loop(0, batches, work, 0)
    for d in range(NZ):
        for half in range(2):
            for e in range(2):
                outs[half * NZ + d][:, e * TB : (e + 1) * TB] = acc_ref[
                    (2 * (d + z) + e) & (RT - 1), half * KH : (half + 1) * KH, :
                ]


def lists_body(coords_ref, live_ref, index_ref, near_ref, far_ref, count_ref):
    z = place_on_mesh(index_ref)[3]

    def enter(slot, found):
        near, far = found
        i = relative_row(coords_ref, slot, z)
        inside = jnp.where((i >= 2 * FAR[0]) & (i < 2 * FAR[-1] + 2), 1, 0)
        far_ref[far] = slot
        near_ref[near] = slot
        return near + 1 - inside, far + inside

    near, far = lax.fori_loop(0, live_ref[0], enter, (jnp.int32(0), jnp.int32(0)))
    count_ref[0] = near
    count_ref[1] = far


def lists_call(coords, live, index):
    return pl.pallas_call(
        lists_body,
        name="lists",
        in_specs=[SMEM_SPEC] * 3,
        out_specs=[SMEM_SPEC] * 3,
        out_shape=[
            jax.ShapeDtypeStruct((NT,), jnp.int32),
            jax.ShapeDtypeStruct((NT,), jnp.int32),
            jax.ShapeDtypeStruct((2,), jnp.int32),
        ],
        compiler_params=pltpu.CompilerParams(vmem_limit_bytes=4 << 20),
    )(coords, live, index)


def sketch_call(coords, live, index, tiles):
    got = pl.pallas_call(
        sketch_body,
        name="sketch",
        in_specs=[SMEM_SPEC] * 3 + [HBM_SPEC],
        out_specs=[VMEM_SPEC] * (2 * NZ + 1),
        scratch_shapes=[
            pltpu.VMEM((CT, K, TB), jnp.bfloat16),
            pltpu.VMEM((RT + 1, K, TB), jnp.float32),
            pltpu.SemaphoreType.DMA((STEPS,)),
        ],
        out_shape=[jax.ShapeDtypeStruct((KH, CH), jnp.float32)] * (2 * NZ)
        + [jax.ShapeDtypeStruct((NT, TB, TB), jnp.bfloat16)],
        compiler_params=pltpu.CompilerParams(vmem_limit_bytes=24 << 20),
    )(coords, live, index, tiles)
    return [got[:NZ], got[NZ : 2 * NZ]], got[2 * NZ]


def split_body(*refs, n, last):
    chunks = refs[: 2 * n]
    split_ref, gram_ref, sum_ref = refs[-3:]

    for c in range(n):
        for half in range(2):
            chunk = chunks[half * n + c]

            def part(g, carry):
                rows = pl.ds(pl.multiple_of(g * 32, 32), 32)
                at = pl.multiple_of(half * KH + g * 32, 32)
                full = chunk[rows, :]
                high = full.astype(jnp.bfloat16)
                low = (full - high.astype(jnp.float32)).astype(jnp.bfloat16)
                for e in range(2):
                    cols = slice(e * TB, (e + 1) * TB)
                    split_ref[2 * c + e, pl.ds(at, 32), :] = high[:, cols]
                    split_ref[2 * c + e, pl.ds(K + at, 32), :] = low[:, cols]
                return carry

            lax.fori_loop(0, KH // 32, part, 0)
    sum_ref[...] = jnp.zeros((2 * K, K), jnp.float32)

    def square(i, carry):
        sum_ref[...] += dot_nt(split_ref[i], split_ref[i, :K, :])
        return carry

    lax.fori_loop(0, 2 * n, square, 0)
    cross = sum_ref[K:, :]
    gram = sum_ref[:K, :] + (cross + cross.T)
    if last:
        gram = refs[2 * n][...] + gram
        for row, col, (i, j) in PACKED:
            gram_ref[row : row + NB, col : col + NB] = gram[i : i + NB, j : j + NB]
    else:
        gram_ref[...] = gram


NB = 64
PACKED = (
    (0, 0, (0, 0)),
    (0, NB, (NB, 0)),
    (NB, 0, (2 * NB, 0)),
    (NB, NB, (NB, NB)),
    (2 * NB, 0, (2 * NB, 2 * NB)),
    (2 * NB, NB, (2 * NB, NB)),
)


def split_call(chunks, carried=()):
    n = len(chunks) // 2
    return pl.pallas_call(
        functools.partial(split_body, n=n, last=bool(carried)),
        name="split_far" if carried else "split_near",
        in_specs=[VMEM_SPEC] * (len(chunks) + len(carried)),
        out_specs=[VMEM_SPEC] * 2,
        scratch_shapes=[pltpu.VMEM((2 * K, K), jnp.float32)],
        out_shape=[
            jax.ShapeDtypeStruct((2 * n, 2 * K, TB), jnp.bfloat16),
            jax.ShapeDtypeStruct((K, 2 * NB) if carried else (K, K), jnp.float32),
        ],
        compiler_params=pltpu.CompilerParams(vmem_limit_bytes=8 << 20),
    )(*chunks, *carried)


def adjoint_body(
    list_ref, coords_ref, count_ref, index_ref, buf_ref, split_ref, *refs, dists, last
):
    if last:
        acc_in, keep_ref, give_ref = refs[:3]
    else:
        acc_out = refs[0]
    acc_ref = refs[-1]
    total = count_ref[1] if last else count_ref[0]
    steps = (total + UNROLL - 1) >> 2
    x, y, core, z = place_on_mesh(index_ref)

    def clear(j, carry):
        acc_ref[j] = acc_in[j] if last else jnp.zeros((K, TB), jnp.float32)
        return carry

    lax.fori_loop(0, CT, clear, 0)

    def work(step, carry):
        for t in range(UNROLL):
            rank = step * UNROLL + t
            slot = list_ref[jnp.minimum(rank, total - 1)]
            i = place_of(relative_row(coords_ref, slot, z), dists)
            j = jnp.where(rank < total, coords_ref[1, slot], CT)
            part = dot_nn(split_ref[i], buf_ref[slot])
            acc_ref[j] += part[:K] + part[K:]
        return carry

    lax.fori_loop(0, steps, work, 0)
    if last:
        mine = pl.multiple_of(core * 128, 128)
        other = pl.multiple_of((1 - core) * 128, 128)

        def place(q, carry):
            one = q >> 2
            two = q & 3
            swap = core == 1
            own = chip_of(x, y, jnp.where(swap, two, one), jnp.where(swap, one, two))
            far = chip_of(x, y, jnp.where(swap, one, two), jnp.where(swap, two, one))
            keep_ref[q] = acc_ref[own, :, pl.ds(mine, 128)]
            give_ref[q] = acc_ref[far, :, pl.ds(other, 128)]
            return carry

        lax.fori_loop(0, CT, place, 0)
    else:

        def save(j, carry):
            acc_out[j] = acc_ref[j]
            return carry

        lax.fori_loop(0, CT, save, 0)


def chip_of(x, y, dx, dy):
    return ((x + dx) & 3) * 4 + ((y + dy) & 3)


def adjoint_call(slots, coords, count, index, held, split, dists, carried=()):
    last = bool(carried)
    part = (CT, K, 128)
    outs = [part, part] if last else [(CT, K, TB)]
    return pl.pallas_call(
        functools.partial(adjoint_body, dists=dists, last=last),
        name="adjoint_far" if last else "adjoint_near",
        in_specs=[SMEM_SPEC] * 4 + [VMEM_SPEC] * (2 + len(carried)),
        out_specs=[VMEM_SPEC] * len(outs),
        scratch_shapes=[pltpu.VMEM((CT + 1, K, TB), jnp.float32)],
        out_shape=[jax.ShapeDtypeStruct(o, jnp.float32) for o in outs],
        compiler_params=pltpu.CompilerParams(vmem_limit_bytes=8 << 20),
    )(slots, coords, count, index, held, split, *carried)


def inverse_factor(block, rows_ref):
    eye = (
        lax.broadcasted_iota(jnp.int32, (NB, NB), 0) == lax.broadcasted_iota(jnp.int32, (NB, NB), 1)
    ).astype(jnp.float32)
    work = jnp.concatenate([eye, block], axis=1)
    first = 0
    for k in range(0, NB, 4):
        o = k - first
        rows = NB - first
        cols = [
            jnp.broadcast_to(work[:, NB + k + m : NB + k + m + 1], (rows, 2 * NB)) for m in range(4)
        ]
        r0, r1, r2, r3 = (work[o + m : o + m + 1] for m in range(4))
        p, q, r = cols[0][o : o + 1], cols[1][o : o + 1], cols[1][o + 1 : o + 2]
        b02, b12, d22 = (cols[2][o + m : o + m + 1] for m in range(3))
        b03, b13, d23, d33 = (cols[3][o + m : o + m + 1] for m in range(4))
        inv = 1.0 / (p * r - q * q)
        h02, h12 = (r * b02 - q * b12) * inv, (p * b12 - q * b02) * inv
        h03, h13 = (r * b03 - q * b13) * inv, (p * b13 - q * b03) * inv
        s22 = d22 - (b02 * h02 + b12 * h12)
        s23 = d23 - (b02 * h03 + b12 * h13)
        s33 = d33 - (b03 * h03 + b13 * h13)
        inv_s = 1.0 / (s22 * s33 - s23 * s23)
        t2 = r2 - (h02 * r0 + h12 * r1)
        t3 = r3 - (h03 * r0 + h13 * r1)
        u2 = (s33 * t2 - s23 * t3) * inv_s
        u3 = (s22 * t3 - s23 * t2) * inv_s
        u0 = (r * r0 - q * r1) * inv - (h02 * u2 + h03 * u3)
        u1 = (p * r1 - q * r0) * inv - (h12 * u2 + h13 * u3)
        ratio = q / p
        rows_ref[k : k + 1, :] = r0 * lax.rsqrt(p)
        rows_ref[k + 1 : k + 2, :] = (r1 - ratio * r0) * lax.rsqrt(r - ratio * q)
        ratio = s23 / s22
        rows_ref[k + 2 : k + 3, :] = t2 * lax.rsqrt(s22)
        rows_ref[k + 3 : k + 4, :] = (t3 - ratio * t2) * lax.rsqrt(s33 - ratio * s23)
        if k + 4 == NB:
            break
        skip = (k + 4) // 8 * 8 - first
        if skip:
            work = work[skip:]
            cols = [c[skip:] for c in cols]
            first += skip
        if (k + 4) % 8:
            below = lax.broadcasted_iota(jnp.int32, work.shape, 0) >= k + 4 - first
            cols = [jnp.where(below, c, 0.0) for c in cols]
        work = work - ((cols[0] * u0 + cols[1] * u1) + (cols[2] * u2 + cols[3] * u3))
    return rows_ref[:, :NB]


def factor_body(packed_ref, out_ref, gram_ref, rows_ref, panel_ref, *, scale):
    n = NB
    for row, col, (i, j) in PACKED:
        block = packed_ref[row : row + n, col : col + n]
        gram_ref[i : i + n, j : j + n] = block
        if i == 2 * n and j == n:
            gram_ref[j : j + n, i : i + n] = block.T
    rows_ref[3, :, :n] = gram_ref[:n, :n]
    out_ref[...] = jnp.zeros((K, K), jnp.float32)

    def block(b, carry):
        w = inverse_factor(rows_ref[3, :, :n], rows_ref.at[b])

        @pl.when(b == 0)
        def _():
            panel = dot_nt(gram_ref[n:, :n], w, HIGHEST)
            panel_ref[...] = panel
            trail = gram_ref[n:, n:] - dot_nt(panel, panel, HIGHEST)
            gram_ref[n:, n:] = trail
            rows_ref[3] = trail[:n]

        @pl.when(b == 1)
        def _():
            l21 = dot_nt(gram_ref[2 * n :, n : 2 * n], w, HIGHEST)
            gram_ref[2 * n :, :n] = l21
            rows_ref[3, :, :n] = gram_ref[2 * n :, 2 * n :] - dot_nt(l21, l21, HIGHEST)

        return carry

    lax.fori_loop(0, 3, block, 0)
    w0, w1, w2 = (rows_ref[b, :, :n] for b in range(3))
    panel = panel_ref[...]
    l21 = gram_ref[2 * n :, :n]
    x10 = -dot_nn(w1, dot_nn(panel[:n], w0, HIGHEST), HIGHEST)
    x21 = -dot_nn(w2, dot_nn(l21, w1, HIGHEST), HIGHEST)
    x20 = -dot_nn(w2, dot_nn(panel[n:], w0, HIGHEST) + dot_nn(l21, x10, HIGHEST), HIGHEST)
    out_ref[:n, :n] = w0 * scale
    out_ref[n : 2 * n, :n] = x10 * scale
    out_ref[n : 2 * n, n : 2 * n] = w1 * scale
    out_ref[2 * n :, :n] = x20 * scale
    out_ref[2 * n :, n : 2 * n] = x21 * scale
    out_ref[2 * n :, 2 * n :] = w2 * scale


def factor_call(packed, scale):
    return pl.pallas_call(
        functools.partial(factor_body, scale=scale),
        name="factor",
        in_specs=[VMEM_SPEC],
        out_specs=VMEM_SPEC,
        scratch_shapes=[
            pltpu.VMEM((K, K), jnp.float32),
            pltpu.VMEM((4, NB, 2 * NB), jnp.float32),
            pltpu.VMEM((2 * NB, NB), jnp.float32),
        ],
        out_shape=jax.ShapeDtypeStruct((K, K), jnp.float32),
        compiler_params=pltpu.CompilerParams(vmem_limit_bytes=4 << 20),
    )(packed)


def apply_body(factor_ref, *refs):
    out_ref = refs[-1]
    both = jnp.concatenate([r[...] for r in refs[:-1]], axis=0)
    out_ref[...] = dot_nn(factor_ref[...], both, HIGHEST)


def apply_call(factor, parts):
    return pl.pallas_call(
        apply_body,
        in_specs=[VMEM_SPEC] * (1 + len(parts)),
        out_specs=VMEM_SPEC,
        out_shape=jax.ShapeDtypeStruct((K, parts[0].shape[1]), jnp.float32),
        compiler_params=pltpu.CompilerParams(vmem_limit_bytes=4 << 20),
    )(factor, *parts)


def shift(x, axis, size, by):
    return lax.ppermute(x, axis, [(i, (i + by) % size) for i in range(size)])


def reduce_z(parts):
    chains = []
    for half, part in enumerate(parts):
        up, down = (4, 3) if half == 0 else (3, 4)
        chains.append([part[up], part[NZ - down], up, down])
    for _ in range(1, 5):
        for chain, part in zip(chains, parts):
            if chain[2]:
                chain[0] = shift(chain[0], "z", NZ, 1)
                chain[2] -= 1
                if chain[2]:
                    chain[0] = chain[0] + part[chain[2]]
            if chain[3]:
                chain[1] = shift(chain[1], "z", NZ, -1)
                chain[3] -= 1
                if chain[3]:
                    chain[1] = chain[1] + part[NZ - chain[3]]
    return [chain[0] + chain[1] + part[0] for chain, part in zip(chains, parts)]


def gather_z(own):
    found = [[mine] + [None] * (NZ - 1) for mine in own]
    for step in range(1, 5):
        for half, got in enumerate(found):
            if step <= (4 if half == 0 else 3):
                got[NZ - step] = shift(got[(NZ - step + 1) % NZ], "z", NZ, 1)
            if step <= (3 if half == 0 else 4):
                got[step] = shift(got[step - 1], "z", NZ, -1)
    return found


def shift_xy(x, by, stage):
    pairs = []
    for i in range(32):
        px, py, core = i // 8, i // 2 % 4, i % 2
        if core == stage:
            px = (px + by) % 4
        else:
            py = (py + by) % 4
        pairs.append((i, (px * 4 + py) * 2 + core))
    return lax.ppermute(x, ("x", "y", "core"), pairs)


def exchange(blocks, stage):
    total = blocks[0]
    for d in (2, 1, 3):
        total = total + shift_xy(blocks[d], d, stage)
    return total


def per_device(tiles, tile_coords, live_counts):
    index = lax.axis_index(("x", "y", "core", "z")).astype(jnp.int32).reshape(1)
    coords = tile_coords.T
    tiles = pltpu.with_memory_space_constraint(tiles, pltpu.HBM)
    parts, held = sketch_call(coords, live_counts, index, tiles)
    near_slots, far_slots, count = lists_call(coords, live_counts, index)
    own = reduce_z(parts)
    found = gather_z(own)
    near = [got[d] for got in found for d in NEAR]
    near_split, near_gram = split_call(near)
    carried = adjoint_call(near_slots, coords, count, index, held, near_split, NEAR)
    rest = [got[d] for got in found for d in FAR]
    far_split, gram = split_call(rest, (near_gram,))
    gram = gram + shift(gram, "core", 2, 1)
    keep, give = adjoint_call(
        far_slots, coords, count, index, held, far_split, FAR, carried
    )
    gram = exchange([gram] * 4, 0)
    blocks = (keep + shift(give, "core", 2, 1)).reshape(4, 4, K, 128)
    gram = exchange([gram] * 4, 1)
    blocks = exchange([blocks[d] for d in range(4)], 0)
    block = exchange([blocks[d] for d in range(4)], 1)
    scale = math.sqrt(RT * TB * 32)
    factor = factor_call(gram, scale)
    range_basis = apply_call(factor, own)
    projected = apply_call(factor, [block])
    return range_basis.T, projected.T[None]


def solution(mesh):
    split = Mesh(mesh.devices.reshape(4, 4, 2, NZ), ("x", "y", "core", "z"))
    row = ("x", "y", "core")
    both = (*row, "z")
    in_specs = (P(both, None, None), P(both, None), P(both))
    out_specs = (P(both, None), P("z", row, None))
    return jax.shard_map(
        per_device, mesh=split, in_specs=in_specs, out_specs=out_specs, check_vma=False
    )
```

```python
import functools
import math

import jax
import jax.numpy as jnp
from jax import lax
from jax.experimental import pallas as pl
from jax.experimental.pallas import tpu as pltpu
from jax.sharding import Mesh
from jax.sharding import PartitionSpec as P

TB = 256
K = 192
RT = 16
CT = 16
NT = 96
NZ = 8
KH = K // 2
CH = RT * TB // NZ
SLOTS = 8
UNROLL = 8
NEAR = (0, 1, 2, 6, 7)
FAR = (3, 4, 5)
STEPS = NT // SLOTS
HIGHEST = lax.Precision.HIGHEST


def dot_nt(a, b, precision=None):
    return lax.dot_general(
        a, b, (((1,), (1,)), ((), ())), precision=precision, preferred_element_type=jnp.float32
    )


def dot_nn(a, b, precision=None):
    return lax.dot_general(
        a, b, (((1,), (0,)), ((), ())), precision=precision, preferred_element_type=jnp.float32
    )


SMEM_SPEC = pl.BlockSpec(memory_space=pltpu.SMEM)
VMEM_SPEC = pl.BlockSpec(memory_space=pltpu.VMEM)
HBM_SPEC = pl.BlockSpec(memory_space=pltpu.HBM)


def place_on_mesh(index_ref):
    index = index_ref[0]
    return (index >> 6) & 3, (index >> 4) & 3, (index >> 3) & 1, index & 7


def relative_row(coords_ref, slot, z):
    return (coords_ref[0, slot] - 2 * z) & (RT - 1)


def place_of(i, dists):
    if dists == FAR:
        return jnp.clip(i - 2 * FAR[0], 0, 2 * len(FAR) - 1)
    return jnp.clip(jnp.where(i >= 12, i - 6, i), 0, 2 * len(NEAR) - 1)


def sketch_body(coords_ref, live_ref, index_ref, tiles_ref, *refs):
    outs = refs[: 2 * NZ]
    buf_ref, omega_ref, acc_ref, sems = refs[2 * NZ :]
    batches = (live_ref[0] + SLOTS - 1) >> 3
    z = place_on_mesh(index_ref)[3]

    def copy(batch):
        part = pl.ds(batch * SLOTS, SLOTS)
        return pltpu.make_async_copy(tiles_ref.at[part], buf_ref.at[part], sems.at[batch])

    def fetch(batch, carry):
        copy(batch).start()
        return carry

    lax.fori_loop(0, batches, fetch, 0)
    k_ids = lax.broadcasted_iota(jnp.int32, (K, TB), 0)
    g_ids = lax.broadcasted_iota(jnp.int32, (K, TB), 1)
    base = (g_ids * K + k_ids) * 747796405

    def fill(j, carry):
        h = base + ((z * CT + j) * (TB * K) * 747796405 + 1442695040)
        h = h ^ (h >> 15)
        h = h * 1103515245 + 12345
        h = h ^ (h >> 13)
        omega_ref[j] = jnp.where((h & 512) == 0, 1.0, -1.0).astype(jnp.bfloat16)
        acc_ref[j] = jnp.zeros((K, TB), jnp.float32)
        return carry

    lax.fori_loop(0, CT, fill, 0)

    def work(batch, carry):
        copy(batch).wait()
        for t in range(SLOTS):
            slot = batch * SLOTS + t
            i = jnp.where(slot < live_ref[0], coords_ref[0, slot], RT)
            acc_ref[i] += dot_nt(omega_ref[coords_ref[1, slot]], buf_ref[slot])
        return carry

    lax.fori_loop(0, batches, work, 0)
    for d in range(NZ):
        for half in range(2):
            for e in range(2):
                outs[half * NZ + d][:, e * TB : (e + 1) * TB] = acc_ref[
                    (2 * (d + z) + e) & (RT - 1), half * KH : (half + 1) * KH, :
                ]


def lists_body(coords_ref, live_ref, index_ref, near_ref, far_ref, count_ref):
    z = place_on_mesh(index_ref)[3]

    def enter(slot, found):
        near, far = found
        i = relative_row(coords_ref, slot, z)
        inside = jnp.where((i >= 2 * FAR[0]) & (i < 2 * FAR[-1] + 2), 1, 0)
        far_ref[far] = slot
        near_ref[near] = slot
        return near + 1 - inside, far + inside

    near, far = lax.fori_loop(0, live_ref[0], enter, (jnp.int32(0), jnp.int32(0)))
    count_ref[0] = near
    count_ref[1] = far


def lists_call(coords, live, index):
    return pl.pallas_call(
        lists_body,
        name="lists",
        in_specs=[SMEM_SPEC] * 3,
        out_specs=[SMEM_SPEC] * 3,
        out_shape=[
            jax.ShapeDtypeStruct((NT,), jnp.int32),
            jax.ShapeDtypeStruct((NT,), jnp.int32),
            jax.ShapeDtypeStruct((2,), jnp.int32),
        ],
        compiler_params=pltpu.CompilerParams(vmem_limit_bytes=4 << 20),
    )(coords, live, index)


def sketch_call(coords, live, index, tiles):
    got = pl.pallas_call(
        sketch_body,
        name="sketch",
        in_specs=[SMEM_SPEC] * 3 + [HBM_SPEC],
        out_specs=[VMEM_SPEC] * (2 * NZ + 1),
        scratch_shapes=[
            pltpu.VMEM((CT, K, TB), jnp.bfloat16),
            pltpu.VMEM((RT + 1, K, TB), jnp.float32),
            pltpu.SemaphoreType.DMA((STEPS,)),
        ],
        out_shape=[jax.ShapeDtypeStruct((KH, CH), jnp.float32)] * (2 * NZ)
        + [jax.ShapeDtypeStruct((NT, TB, TB), jnp.bfloat16)],
        compiler_params=pltpu.CompilerParams(vmem_limit_bytes=24 << 20),
    )(coords, live, index, tiles)
    return [got[:NZ], got[NZ : 2 * NZ]], got[2 * NZ]


def split_body(*refs, n, last):
    chunks = refs[: 2 * n]
    split_ref, gram_ref, sum_ref = refs[-3:]

    for c in range(n):
        for half in range(2):
            chunk = chunks[half * n + c]

            def part(g, carry):
                rows = pl.ds(pl.multiple_of(g * 32, 32), 32)
                at = pl.multiple_of(half * KH + g * 32, 32)
                full = chunk[rows, :]
                high = full.astype(jnp.bfloat16)
                low = (full - high.astype(jnp.float32)).astype(jnp.bfloat16)
                for e in range(2):
                    cols = slice(e * TB, (e + 1) * TB)
                    split_ref[2 * c + e, pl.ds(at, 32), :] = high[:, cols]
                    split_ref[2 * c + e, pl.ds(K + at, 32), :] = low[:, cols]
                return carry

            lax.fori_loop(0, KH // 32, part, 0)
    sum_ref[...] = jnp.zeros((2 * K, K), jnp.float32)

    def square(i, carry):
        sum_ref[...] += dot_nt(split_ref[i], split_ref[i, :K, :])
        return carry

    lax.fori_loop(0, 2 * n, square, 0)
    cross = sum_ref[K:, :]
    gram = sum_ref[:K, :] + (cross + cross.T)
    if last:
        gram = refs[2 * n][...] + gram
        for row, col, (i, j) in PACKED:
            gram_ref[row : row + NB, col : col + NB] = gram[i : i + NB, j : j + NB]
    else:
        gram_ref[...] = gram


NB = 64
PACKED = (
    (0, 0, (0, 0)),
    (0, NB, (NB, 0)),
    (NB, 0, (2 * NB, 0)),
    (NB, NB, (NB, NB)),
    (2 * NB, 0, (2 * NB, 2 * NB)),
    (2 * NB, NB, (2 * NB, NB)),
)


def split_call(chunks, carried=()):
    n = len(chunks) // 2
    return pl.pallas_call(
        functools.partial(split_body, n=n, last=bool(carried)),
        name="split_far" if carried else "split_near",
        in_specs=[VMEM_SPEC] * (len(chunks) + len(carried)),
        out_specs=[VMEM_SPEC] * 2,
        scratch_shapes=[pltpu.VMEM((2 * K, K), jnp.float32)],
        out_shape=[
            jax.ShapeDtypeStruct((2 * n, 2 * K, TB), jnp.bfloat16),
            jax.ShapeDtypeStruct((K, 2 * NB) if carried else (K, K), jnp.float32),
        ],
        compiler_params=pltpu.CompilerParams(vmem_limit_bytes=8 << 20),
    )(*chunks, *carried)


def adjoint_body(
    list_ref, coords_ref, count_ref, index_ref, buf_ref, split_ref, *refs, dists, last
):
    if last:
        acc_in, keep_ref, give_ref = refs[:3]
    else:
        acc_out = refs[0]
    acc_ref = refs[-1]
    total = count_ref[1] if last else count_ref[0]
    steps = (total + UNROLL - 1) >> 3
    x, y, core, z = place_on_mesh(index_ref)

    def clear(j, carry):
        acc_ref[j] = acc_in[j] if last else jnp.zeros((K, TB), jnp.float32)
        return carry

    lax.fori_loop(0, CT, clear, 0)

    def work(step, carry):
        for t in range(UNROLL):
            rank = step * UNROLL + t
            slot = list_ref[jnp.minimum(rank, total - 1)]
            i = place_of(relative_row(coords_ref, slot, z), dists)
            j = jnp.where(rank < total, coords_ref[1, slot], CT)
            part = dot_nn(split_ref[i], buf_ref[slot])
            acc_ref[j] += part[:K] + part[K:]
        return carry

    lax.fori_loop(0, steps, work, 0)
    if last:
        mine = pl.multiple_of(core * 128, 128)
        other = pl.multiple_of((1 - core) * 128, 128)

        def place(q, carry):
            one = q >> 2
            two = q & 3
            swap = core == 1
            own = chip_of(x, y, jnp.where(swap, two, one), jnp.where(swap, one, two))
            far = chip_of(x, y, jnp.where(swap, one, two), jnp.where(swap, two, one))
            keep_ref[q] = acc_ref[own, :, pl.ds(mine, 128)]
            give_ref[q] = acc_ref[far, :, pl.ds(other, 128)]
            return carry

        lax.fori_loop(0, CT, place, 0)
    else:

        def save(j, carry):
            acc_out[j] = acc_ref[j]
            return carry

        lax.fori_loop(0, CT, save, 0)


def chip_of(x, y, dx, dy):
    return ((x + dx) & 3) * 4 + ((y + dy) & 3)


def adjoint_call(slots, coords, count, index, held, split, dists, carried=()):
    last = bool(carried)
    part = (CT, K, 128)
    outs = [part, part] if last else [(CT, K, TB)]
    return pl.pallas_call(
        functools.partial(adjoint_body, dists=dists, last=last),
        name="adjoint_far" if last else "adjoint_near",
        in_specs=[SMEM_SPEC] * 4 + [VMEM_SPEC] * (2 + len(carried)),
        out_specs=[VMEM_SPEC] * len(outs),
        scratch_shapes=[pltpu.VMEM((CT + 1, K, TB), jnp.float32)],
        out_shape=[jax.ShapeDtypeStruct(o, jnp.float32) for o in outs],
        compiler_params=pltpu.CompilerParams(vmem_limit_bytes=8 << 20),
    )(slots, coords, count, index, held, split, *carried)


def inverse_factor(block, rows_ref):
    eye = (
        lax.broadcasted_iota(jnp.int32, (NB, NB), 0) == lax.broadcasted_iota(jnp.int32, (NB, NB), 1)
    ).astype(jnp.float32)
    work = jnp.concatenate([eye, block], axis=1)
    first = 0
    for k in range(0, NB, 4):
        o = k - first
        rows = NB - first
        cols = [
            jnp.broadcast_to(work[:, NB + k + m : NB + k + m + 1], (rows, 2 * NB)) for m in range(4)
        ]
        r0, r1, r2, r3 = (work[o + m : o + m + 1] for m in range(4))
        p, q, r = cols[0][o : o + 1], cols[1][o : o + 1], cols[1][o + 1 : o + 2]
        b02, b12, d22 = (cols[2][o + m : o + m + 1] for m in range(3))
        b03, b13, d23, d33 = (cols[3][o + m : o + m + 1] for m in range(4))
        inv = 1.0 / (p * r - q * q)
        h02, h12 = (r * b02 - q * b12) * inv, (p * b12 - q * b02) * inv
        h03, h13 = (r * b03 - q * b13) * inv, (p * b13 - q * b03) * inv
        s22 = d22 - (b02 * h02 + b12 * h12)
        s23 = d23 - (b02 * h03 + b12 * h13)
        s33 = d33 - (b03 * h03 + b13 * h13)
        inv_s = 1.0 / (s22 * s33 - s23 * s23)
        t2 = r2 - (h02 * r0 + h12 * r1)
        t3 = r3 - (h03 * r0 + h13 * r1)
        u2 = (s33 * t2 - s23 * t3) * inv_s
        u3 = (s22 * t3 - s23 * t2) * inv_s
        u0 = (r * r0 - q * r1) * inv - (h02 * u2 + h03 * u3)
        u1 = (p * r1 - q * r0) * inv - (h12 * u2 + h13 * u3)
        ratio = q / p
        rows_ref[k : k + 1, :] = r0 * lax.rsqrt(p)
        rows_ref[k + 1 : k + 2, :] = (r1 - ratio * r0) * lax.rsqrt(r - ratio * q)
        ratio = s23 / s22
        rows_ref[k + 2 : k + 3, :] = t2 * lax.rsqrt(s22)
        rows_ref[k + 3 : k + 4, :] = (t3 - ratio * t2) * lax.rsqrt(s33 - ratio * s23)
        if k + 4 == NB:
            break
        skip = (k + 4) // 8 * 8 - first
        if skip:
            work = work[skip:]
            cols = [c[skip:] for c in cols]
            first += skip
        if (k + 4) % 8:
            below = lax.broadcasted_iota(jnp.int32, work.shape, 0) >= k + 4 - first
            cols = [jnp.where(below, c, 0.0) for c in cols]
        work = work - ((cols[0] * u0 + cols[1] * u1) + (cols[2] * u2 + cols[3] * u3))
    return rows_ref[:, :NB]


def factor_body(packed_ref, out_ref, gram_ref, rows_ref, panel_ref, *, scale):
    n = NB
    for row, col, (i, j) in PACKED:
        block = packed_ref[row : row + n, col : col + n]
        gram_ref[i : i + n, j : j + n] = block
        if i == 2 * n and j == n:
            gram_ref[j : j + n, i : i + n] = block.T
    rows_ref[3, :, :n] = gram_ref[:n, :n]
    out_ref[...] = jnp.zeros((K, K), jnp.float32)

    def block(b, carry):
        w = inverse_factor(rows_ref[3, :, :n], rows_ref.at[b])

        @pl.when(b == 0)
        def _():
            panel = dot_nt(gram_ref[n:, :n], w, HIGHEST)
            panel_ref[...] = panel
            trail = gram_ref[n:, n:] - dot_nt(panel, panel, HIGHEST)
            gram_ref[n:, n:] = trail
            rows_ref[3] = trail[:n]

        @pl.when(b == 1)
        def _():
            l21 = dot_nt(gram_ref[2 * n :, n : 2 * n], w, HIGHEST)
            gram_ref[2 * n :, :n] = l21
            rows_ref[3, :, :n] = gram_ref[2 * n :, 2 * n :] - dot_nt(l21, l21, HIGHEST)

        return carry

    lax.fori_loop(0, 3, block, 0)
    w0, w1, w2 = (rows_ref[b, :, :n] for b in range(3))
    panel = panel_ref[...]
    l21 = gram_ref[2 * n :, :n]
    x10 = -dot_nn(w1, dot_nn(panel[:n], w0, HIGHEST), HIGHEST)
    x21 = -dot_nn(w2, dot_nn(l21, w1, HIGHEST), HIGHEST)
    x20 = -dot_nn(w2, dot_nn(panel[n:], w0, HIGHEST) + dot_nn(l21, x10, HIGHEST), HIGHEST)
    out_ref[:n, :n] = w0 * scale
    out_ref[n : 2 * n, :n] = x10 * scale
    out_ref[n : 2 * n, n : 2 * n] = w1 * scale
    out_ref[2 * n :, :n] = x20 * scale
    out_ref[2 * n :, n : 2 * n] = x21 * scale
    out_ref[2 * n :, 2 * n :] = w2 * scale


def factor_call(packed, scale):
    return pl.pallas_call(
        functools.partial(factor_body, scale=scale),
        name="factor",
        in_specs=[VMEM_SPEC],
        out_specs=VMEM_SPEC,
        scratch_shapes=[
            pltpu.VMEM((K, K), jnp.float32),
            pltpu.VMEM((4, NB, 2 * NB), jnp.float32),
            pltpu.VMEM((2 * NB, NB), jnp.float32),
        ],
        out_shape=jax.ShapeDtypeStruct((K, K), jnp.float32),
        compiler_params=pltpu.CompilerParams(vmem_limit_bytes=4 << 20),
    )(packed)


def apply_body(factor_ref, *refs):
    out_ref = refs[-1]
    both = jnp.concatenate([r[...] for r in refs[:-1]], axis=0)
    out_ref[...] = dot_nn(factor_ref[...], both, HIGHEST)


def apply_call(factor, parts):
    return pl.pallas_call(
        apply_body,
        in_specs=[VMEM_SPEC] * (1 + len(parts)),
        out_specs=VMEM_SPEC,
        out_shape=jax.ShapeDtypeStruct((K, parts[0].shape[1]), jnp.float32),
        compiler_params=pltpu.CompilerParams(vmem_limit_bytes=4 << 20),
    )(factor, *parts)


def shift(x, axis, size, by):
    return lax.ppermute(x, axis, [(i, (i + by) % size) for i in range(size)])


def reduce_z(parts):
    chains = []
    for half, part in enumerate(parts):
        up, down = (4, 3) if half == 0 else (3, 4)
        chains.append([part[up], part[NZ - down], up, down])
    for _ in range(1, 5):
        for chain, part in zip(chains, parts):
            if chain[2]:
                chain[0] = shift(chain[0], "z", NZ, 1)
                chain[2] -= 1
                if chain[2]:
                    chain[0] = chain[0] + part[chain[2]]
            if chain[3]:
                chain[1] = shift(chain[1], "z", NZ, -1)
                chain[3] -= 1
                if chain[3]:
                    chain[1] = chain[1] + part[NZ - chain[3]]
    return [chain[0] + chain[1] + part[0] for chain, part in zip(chains, parts)]


def gather_z(own):
    found = [[mine] + [None] * (NZ - 1) for mine in own]
    for step in range(1, 5):
        for half, got in enumerate(found):
            if step <= (4 if half == 0 else 3):
                got[NZ - step] = shift(got[(NZ - step + 1) % NZ], "z", NZ, 1)
            if step <= (3 if half == 0 else 4):
                got[step] = shift(got[step - 1], "z", NZ, -1)
    return found


def shift_xy(x, by, stage):
    pairs = []
    for i in range(32):
        px, py, core = i // 8, i // 2 % 4, i % 2
        if core == stage:
            px = (px + by) % 4
        else:
            py = (py + by) % 4
        pairs.append((i, (px * 4 + py) * 2 + core))
    return lax.ppermute(x, ("x", "y", "core"), pairs)


def exchange(blocks, stage):
    total = blocks[0]
    for d in (2, 1, 3):
        total = total + shift_xy(blocks[d], d, stage)
    return total


def per_device(tiles, tile_coords, live_counts):
    index = lax.axis_index(("x", "y", "core", "z")).astype(jnp.int32).reshape(1)
    coords = pltpu.with_memory_space_constraint(tile_coords.T, pltpu.HBM)
    tiles = pltpu.with_memory_space_constraint(tiles, pltpu.HBM)
    parts, held = sketch_call(coords, live_counts, index, tiles)
    near_slots, far_slots, count = lists_call(coords, live_counts, index)
    own = reduce_z(parts)
    found = gather_z(own)
    near = [got[d] for got in found for d in NEAR]
    near_split, near_gram = split_call(near)
    carried = adjoint_call(near_slots, coords, count, index, held, near_split, NEAR)
    rest = [got[d] for got in found for d in FAR]
    far_split, gram = split_call(rest, (near_gram,))
    gram = gram + shift(gram, "core", 2, 1)
    keep, give = adjoint_call(
        far_slots, coords, count, index, held, far_split, FAR, carried
    )
    gram = exchange([gram] * 4, 0)
    blocks = (keep + shift(give, "core", 2, 1)).reshape(4, 4, K, 128)
    gram = exchange([gram] * 4, 1)
    blocks = exchange([blocks[d] for d in range(4)], 0)
    block = exchange([blocks[d] for d in range(4)], 1)
    scale = math.sqrt(RT * TB * 32)
    factor = factor_call(gram, scale)
    range_basis = apply_call(factor, own)
    projected = apply_call(factor, [block])
    return range_basis.T, projected.T[None]


def solution(mesh):
    split = Mesh(mesh.devices.reshape(4, 4, 2, NZ), ("x", "y", "core", "z"))
    row = ("x", "y", "core")
    both = (*row, "z")
    in_specs = (P(both, None, None), P(both, None), P(both))
    out_specs = (P(both, None), P("z", row, None))
    return jax.shard_map(
        per_device, mesh=split, in_specs=in_specs, out_specs=out_specs, check_vma=False
    )
```
